32 devices in a mesh: section: 2 (over core), seq: 4 (over z), fsdp: 4 (over y, x).
Axes of the slice: x: 2, y: 2, z: 4, core: 2. Of those that a mesh axis runs over, the one named last changes fastest.
Arguments:
- inputs: float32 [2, 4, 512, 768], P(None, 'fsdp', 'seq'), may hold values from -6 to 6
- out_grad: float32 [2, 4, 512, 768], P(None, 'fsdp', 'seq'), may hold values from -6 to 6
- norm_gain: bfloat16 [2, 768], P('section', 'fsdp'), may hold values from 0.099609375 to 1.8984375
- input_weight: bfloat16 [2, 768, 3328], P('section', 'fsdp'), may hold values from -0.21875 to 0.21875
- conv_weight: bfloat16 [2, 4, 1792], P('section', None, 'fsdp'), may hold values from -3 to 3
- conv_bias: bfloat16 [2, 1792], P('section', 'fsdp'), may hold values from -3 to 3
- skip_gain: bfloat16 [2, 24], P('section', 'fsdp'), may hold values from 1 to 4
- gate_gain: bfloat16 [2, 1536], P('section', 'fsdp'), may hold values from 0.099609375 to 1.8984375
- out_weight: bfloat16 [2, 1536, 768], P('section', 'fsdp'), may hold values from -0.15625 to 0.15625
- step_codes: int32 [2, 2, 4, 512, 24], P('section', None, 'fsdp', 'seq'), may hold values from 128 to 512
- decay_codes: int32 [2, 2, 4, 512, 24], P('section', None, 'fsdp', 'seq'), may hold values from 2 to 45000, as said below
Outputs:
- section_outputs: float32 [2, 2, 4, 512, 768], P('section', None, 'fsdp', 'seq')
- section_input_grads: float32 [2, 2, 4, 512, 768], P('section', None, 'fsdp', 'seq')
- norm_gain_grad: float32 [2, 768], P('section', 'fsdp')
- in_weight_grad: float32 [2, 768, 3328], P('section', 'fsdp')
- conv_weight_grad: float32 [2, 4, 1792], P('section', None, 'fsdp')
- conv_bias_grad: float32 [2, 1792], P('section', 'fsdp')
- skip_gain_grad: float32 [2, 24], P('section', 'fsdp')
- gate_gain_grad: float32 [2, 1536], P('section', 'fsdp')
- out_weight_grad: float32 [2, 1536, 768], P('section', 'fsdp')
The draws below stay inside these ranges and needn't reach their ends.
Inputs may be any that keep to these rules, and one draw needn't show every extreme that they name: `decay_codes`: codes are positive.
All inputs are finite; a program needn't handle non-finite values.
Results may differ from the reference program's by a relative error of at most 0.012.
Values may be sent and summed in bfloat16 or wider, within the bound.
A program may use at most 256 MiB of HBM per device.

```python
import math
from functools import partial
import jax
import jax.numpy as jnp
from jax import lax

D = 768
DI = 1536
HEADS = 24
HEAD_DIM = 64
STATE = 128
CONV = 4
MICRO = 2
TOK_DEV = 128
LAYERS = 2
SEQS = 4
L = 512
PROJ = 3328
DC = 1792


def draw_decay_codes(key, part):
    subkeys = jax.random.split(key, 7)
    blocks = L // TOK_DEV
    fast_heads = jax.random.randint(subkeys[0], (LAYERS, 1, 1, 1, 1, HEADS), 0, 5) < 2
    fast_base = jax.random.randint(subkeys[1], (LAYERS, 1, 1, 1, 1, HEADS), 1300, 2200)
    slow_base = jax.random.randint(subkeys[2], (LAYERS, 1, 1, 1, 1, HEADS), 2, 5)
    head_base = jnp.where(fast_heads, fast_base, slow_base)
    device_factor = jax.random.randint(subkeys[3], (LAYERS, MICRO, SEQS, blocks, 1, HEADS), 2, 6)
    token_factor = jax.random.randint(subkeys[4], (LAYERS, MICRO, SEQS, blocks, TOK_DEV, HEADS), 2, 5)
    attenuation_multipliers = head_base * device_factor * token_factor // 4
    attenuation_multipliers = attenuation_multipliers.reshape(LAYERS, MICRO, SEQS, L, HEADS)
    location_series = jax.random.randint(subkeys[5], (LAYERS, MICRO, SEQS, 1, 3), 0, L)
    drawn = jax.random.randint(subkeys[6], (LAYERS, MICRO, SEQS, 1, 3), 15000, 45000)
    which = lax.broadcasted_iota(jnp.int32, (LAYERS, MICRO, SEQS, 1, 3), 4)
    quantity_series = jnp.where(which == 0, 45000, drawn)
    sequence_indices = lax.broadcasted_iota(jnp.int32, (LAYERS, MICRO, SEQS, L, 3), 3)
    clustered_sets = jnp.max(jnp.where(sequence_indices == location_series, quantity_series, 0), axis=-1)
    return jnp.maximum(attenuation_multipliers, clustered_sets[..., None]).astype(jnp.int32)


def plant(values, own_key, least, top_value):
    longest = values.shape.index(max(values.shape))
    spots = []
    for shift in (0, 1):
        where = [jax.random.randint(jax.random.fold_in(own_key, axis), (), 0, length) for axis, length in enumerate(values.shape)]
        where[longest] = (where[longest] + shift) % values.shape[longest]
        spots.append(tuple(where))
    return values.at[spots[0]].set(least).at[spots[1]].set(top_value)


def steps_of(stream_key, shape, cuts, least, high):
    level, own = 1.0, jax.random.fold_in(stream_key, 6)
    for axis_at, blocks in cuts:
        draws = jnp.exp(jax.random.uniform(jax.random.fold_in(own, axis_at), (blocks,), jnp.float32, least / len(cuts), high / len(cuts)))
        level = level * jnp.repeat(draws, shape[axis_at] // blocks).reshape([-1 if axis == axis_at else 1 for axis in range(len(shape))])
    return level


def scatter_about(stream_key, dims, spread, bound, cuts=(), dtype=jnp.bfloat16):
    level = steps_of(stream_key, dims, cuts, -0.22, 0.18) if cuts else 1.0
    values = jax.random.normal(stream_key, dims, jnp.float32) * spread * level
    return jnp.minimum(jnp.maximum(values, -bound), bound).astype(dtype)


def setup_inputs(seed: int = 0) -> dict:
    splits = jax.random.split(jax.random.key(seed), 12)
    inputs = scatter_about(splits[0], (MICRO, SEQS, L, D), 1.0, 6.0, ((1, 4), (2, 4)), jnp.float32)
    out_grad = scatter_about(splits[1], (MICRO, SEQS, L, D), 1.0, 6.0, ((1, 4), (2, 4)), jnp.float32)
    norm_gain = jnp.clip(1.0 + 0.18 * jax.random.normal(splits[2], (LAYERS, D), jnp.float32), 0.099609375, 1.8984375).astype(jnp.bfloat16)
    input_weight = scatter_about(splits[3], (LAYERS, D, PROJ), D ** -0.5, 0.21875, ((0, 2), (1, 4)))
    conv_weight = scatter_about(splits[4], (LAYERS, CONV, DC), CONV ** -0.5, 3.0, ((0, 2), (2, 4)))
    conv_bias = scatter_about(splits[5], (LAYERS, DC), 0.5, 3.0, ((0, 2), (1, 4)))
    skip_gain = jnp.clip(jnp.exp(math.log(4.0) - 1.3862944 * jax.random.uniform(splits[6], (LAYERS, HEADS), jnp.float32) ** steps_of(splits[6], (LAYERS, HEADS), ((0, 2), (1, 4)), -0.2, 0.2)), 1.0, 4.0).astype(jnp.bfloat16)
    gate_gain = jnp.clip(1.0 + 0.18 * jax.random.normal(splits[7], (LAYERS, DI), jnp.float32), 0.099609375, 1.8984375).astype(jnp.bfloat16)
    out_weight = scatter_about(splits[8], (LAYERS, DI, D), DI ** -0.5, 0.15625, ((0, 2), (1, 4)))
    step_codes = plant(jax.random.randint(splits[9], (LAYERS, MICRO, SEQS, L, HEADS), 128, 513), jax.random.fold_in(splits[9], 1), 128, 512).astype(jnp.int32)
    decay_codes = draw_decay_codes(jax.random.fold_in(splits[11], 71), 0)
    return {"inputs": inputs, "out_grad": out_grad, "norm_gain": norm_gain, "input_weight": input_weight, "conv_weight": conv_weight, "conv_bias": conv_bias, "skip_gain": skip_gain, "gate_gain": gate_gain, "out_weight": out_weight, "step_codes": step_codes, "decay_codes": decay_codes}


EPSILON = 1e-05
STEP_SCALE = 256.0
DECAY_SCALE = 65536.0
HIGHEST = lax.Precision.HIGHEST

def norm_input(hidden, gain_vector):
    inverse_rms = lax.rsqrt(lax.optimization_barrier(jnp.mean(hidden * hidden, axis=-1, keepdims=True)) + EPSILON)
    return hidden * inverse_rms * gain_vector

def gated_norm(mixer_out, gate_outputs, gain_vector):
    gated_products = mixer_out * jax.nn.silu(gate_outputs)
    inverse_rms = lax.rsqrt(lax.optimization_barrier(jnp.mean(gated_products * gated_products, axis=-1, keepdims=True)) + EPSILON)
    return gated_products * inverse_rms * gain_vector

def conv_silu(before, current, kernel, offset):
    extended = jnp.concatenate([before, current], axis=0)
    length = current.shape[0]
    summed = offset[None, :] + kernel[0][None, :] * extended[0:length]
    for shift_row in range(1, kernel.shape[0]):
        summed = summed + kernel[shift_row][None, :] * extended[shift_row:shift_row + length]
    return jax.nn.silu(summed)

def split_mixer(conv_part):
    length = conv_part.shape[0]
    head_values = conv_part[:, :DI].reshape(length, HEADS, HEAD_DIM)
    input_keys = conv_part[:, DI:DI + STATE]
    output_queries = conv_part[:, DI + STATE:]
    return (head_values, input_keys, output_queries)

def step_and_decay(step_block, decay_block):
    step_sizes = step_block.astype(jnp.float32) / STEP_SCALE
    cumulative = jnp.cumsum(-decay_block.astype(jnp.float32) / DECAY_SCALE, axis=0)
    return (step_sizes, cumulative)

def block_summary(head_values, input_keys, step_sizes, cumulative):
    to_end = jnp.exp(cumulative[-1][None, :] - cumulative) * step_sizes
    return jnp.einsum('sh,shp,sn->hpn', to_end, head_values, input_keys, precision=HIGHEST)

def block_output(head_values, input_keys, output_queries, step_sizes, cumulative, entering, skip_weights):
    length = head_values.shape[0]
    later = lax.broadcasted_iota(jnp.int32, (length, length), 0)
    earlier = lax.broadcasted_iota(jnp.int32, (length, length), 1)
    causal = (later >= earlier)[None, :, :]
    cum_heads = cumulative.T
    dispersion_width = cum_heads[:, :, None] - cum_heads[:, None, :]
    decays = jnp.where(causal, jnp.exp(jnp.where(causal, dispersion_width, 0.0)), 0.0)
    scores = jnp.dot(output_queries, input_keys.T, precision=HIGHEST)
    coupling = decays * scores[None, :, :] * step_sizes.T[:, None, :]
    within = jnp.einsum('hts,shp->thp', coupling, head_values, precision=HIGHEST)
    carried = jnp.exp(cumulative)[:, :, None] * jnp.einsum('tn,hpn->thp', output_queries, entering, precision=HIGHEST)
    return within + carried + skip_weights[None, :, None] * head_values

def mixer_blocks(head_values, input_keys, output_queries, skip_weights, step_sizes, cumulative, entering):
    mixed = jax.vmap(block_output, in_axes=(0, 0, 0, 0, 0, 0, None))(head_values, input_keys, output_queries, step_sizes, cumulative, entering, skip_weights)
    summaries = jax.vmap(block_summary)(head_values, input_keys, step_sizes, cumulative)
    return (mixed, summaries)

def sequence_parts(hidden, params, step_rows, decay_rows):
    normed = norm_input(hidden, params[1].astype(jnp.float32)).astype(jnp.bfloat16)
    projected = jnp.dot(normed, params[0], preferred_element_type=jnp.float32)
    gate_outputs = projected[:, :DI]
    mixer_rows = projected[:, DI:]
    before = jnp.zeros((CONV - 1, mixer_rows.shape[1]), jnp.float32)
    conv_part = conv_silu(before, mixer_rows, params[2].astype(jnp.float32), params[3].astype(jnp.float32))
    blocks = hidden.shape[0] // TOK_DEV
    head_values, input_keys, output_queries = split_mixer(conv_part)
    head_values = head_values.reshape(blocks, TOK_DEV, HEADS, HEAD_DIM)
    input_keys = input_keys.reshape(blocks, TOK_DEV, STATE)
    output_queries = output_queries.reshape(blocks, TOK_DEV, STATE)
    step_sizes, cumulative = jax.vmap(step_and_decay)(step_rows.reshape(blocks, TOK_DEV, HEADS), decay_rows.reshape(blocks, TOK_DEV, HEADS))
    summaries = jax.vmap(block_summary)(head_values, input_keys, step_sizes, cumulative)

    def advance(state_now, pieces):
        return (jnp.exp(pieces[0])[:, None, None] * state_now + pieces[1], state_now)
    _, entering = lax.scan(advance, jnp.zeros(summaries.shape[1:], jnp.float32), (cumulative[:, -1], summaries))
    return (normed, gate_outputs, mixer_rows, before, head_values, input_keys, output_queries, step_sizes, cumulative, entering)

def forward_sequence(params, sequence_item):
    hidden, step_rows, decay_rows = sequence_item
    parts = sequence_parts(hidden, params, step_rows, decay_rows)
    normed, gate_outputs, mixer_rows, before, head_values, input_keys, output_queries, step_sizes, cumulative, entering = parts
    mixed, _ = mixer_blocks(head_values, input_keys, output_queries, params[4].astype(jnp.float32), step_sizes, cumulative, entering)
    mixer_out = mixed.reshape(hidden.shape[0], DI)
    normed_out = gated_norm(mixer_out, gate_outputs, params[5].astype(jnp.float32)).astype(jnp.bfloat16)
    return hidden + jnp.dot(normed_out, params[6], preferred_element_type=jnp.float32)

def backward_sequence(params, sequence_item):
    hidden, out_cot, step_rows, decay_rows = sequence_item
    length = hidden.shape[0]
    parts = sequence_parts(hidden, params, step_rows, decay_rows)
    normed, gate_outputs, mixer_rows, before, head_values, input_keys, output_queries, step_sizes, cumulative, entering = parts

    def mixer_fn(values_in, keys_in, queries_in, skip_in):
        return mixer_blocks(values_in, keys_in, queries_in, skip_in, step_sizes, cumulative, entering)
    (mixed, _), mixer_vjp = jax.vjp(mixer_fn, head_values, input_keys, output_queries, params[4].astype(jnp.float32))
    mixer_out = mixed.reshape(length, DI)
    normed_out, norm_vjp = jax.vjp(gated_norm, mixer_out, gate_outputs, params[5].astype(jnp.float32))
    out_rounded = normed_out.astype(jnp.bfloat16)
    cot_rounded = out_cot.astype(jnp.bfloat16)
    grad_out_weight = jnp.dot(out_rounded.T, cot_rounded, preferred_element_type=jnp.float32)
    grad_normed_out = jnp.dot(cot_rounded, params[6].T, preferred_element_type=jnp.float32)
    grad_mixer, grad_gate, grad_gate_gain = norm_vjp(grad_normed_out)
    grad_heads = grad_mixer.reshape(head_values.shape)
    local_entry = jnp.einsum('bth,bthp,btn->bhpn', jnp.exp(cumulative), grad_heads, output_queries, precision=HIGHEST)

    def retreat(carry_grad, pieces):
        return (pieces[1] + jnp.exp(pieces[0])[:, None, None] * carry_grad, carry_grad)
    _, leaving = lax.scan(retreat, jnp.zeros(local_entry.shape[1:], jnp.float32), (cumulative[:, -1], local_entry), reverse=True)
    grad_values, grad_keys, grad_queries, grad_skip = mixer_vjp((grad_heads, leaving))
    grad_conv = jnp.concatenate([grad_values.reshape(length, DI), grad_keys.reshape(length, STATE), grad_queries.reshape(length, STATE)], axis=1)

    def conv_fn(rows_in, kernel_in, offset_in):
        return conv_silu(before, rows_in, kernel_in, offset_in)
    _, conv_vjp = jax.vjp(conv_fn, mixer_rows, params[2].astype(jnp.float32), params[3].astype(jnp.float32))
    grad_rows, grad_kernel, grad_offset = conv_vjp(grad_conv)
    grad_projected = jnp.concatenate([grad_gate, grad_rows], axis=1).astype(jnp.bfloat16)
    grad_in_weight = jnp.dot(normed.T, grad_projected, preferred_element_type=jnp.float32)
    grad_normed = jnp.dot(grad_projected, params[0].T, preferred_element_type=jnp.float32)
    _, input_vjp = jax.vjp(norm_input, hidden, params[1].astype(jnp.float32))
    grad_hidden, grad_norm_gain = input_vjp(grad_normed)
    pieces = (grad_in_weight, grad_norm_gain, grad_kernel, grad_offset, grad_skip, grad_gate_gain, grad_out_weight)
    return (out_cot + grad_hidden, pieces)

def accumulate(params, totals, sequence_item):
    grad_hidden, pieces = backward_sequence(params, sequence_item)
    return (tuple((running + added for running, added in zip(totals, pieces))), grad_hidden)

def reference(inputs, out_grad, norm_gain, input_weight, conv_weight, conv_bias, skip_gain, gate_gain, out_weight, step_codes, decay_codes):
    sequences = inputs.shape[0] * inputs.shape[1]
    length = inputs.shape[2]
    current = inputs.reshape(sequences, length, D)
    layer_inputs = []
    layer_outputs = []
    all_params = []
    for layer_index in range(LAYERS):
        params = (input_weight[layer_index], norm_gain[layer_index], conv_weight[layer_index], conv_bias[layer_index], skip_gain[layer_index], gate_gain[layer_index], out_weight[layer_index])
        all_params.append(params)
        step_rows = step_codes[layer_index].reshape(sequences, length, HEADS)
        decay_rows = decay_codes[layer_index].reshape(sequences, length, HEADS)
        layer_inputs.append(current)
        current = lax.map(partial(forward_sequence, params), (current, step_rows, decay_rows))
        layer_outputs.append(current)
    adjoint_vector = out_grad.reshape(sequences, length, D)
    input_grads = [None] * LAYERS
    weight_grads = [None] * LAYERS
    for layer_index in range(LAYERS - 1, -1, -1):
        params = all_params[layer_index]
        step_rows = step_codes[layer_index].reshape(sequences, length, HEADS)
        decay_rows = decay_codes[layer_index].reshape(sequences, length, HEADS)
        zero_totals = tuple((jnp.zeros(weight.shape, jnp.float32) for weight in params))
        totals, adjoint_vector = lax.scan(partial(accumulate, params), zero_totals, (layer_inputs[layer_index], adjoint_vector, step_rows, decay_rows))
        input_grads[layer_index] = adjoint_vector
        weight_grads[layer_index] = totals
    shape_out = (LAYERS, MICRO, SEQS, length, D)
    section_outputs = jnp.stack(layer_outputs).reshape(shape_out)
    section_input_grads = jnp.stack(input_grads).reshape(shape_out)
    stacked = [jnp.stack([weight_grads[layer_index][member] for layer_index in range(LAYERS)]) for member in range(7)]
    return (section_outputs, section_input_grads, stacked[1], stacked[0], stacked[2], stacked[3], stacked[4], stacked[5], stacked[6])
```

```python
import types

import jax
import jax.numpy as jnp
from jax import lax
from jax.experimental import pallas as pl
from jax.experimental.pallas import tpu as pltpu
from jax.sharding import PartitionSpec as P

EPSILON = 1e-05
STEP_SCALE = 256.0
DECAY_SCALE = 65536.0
HIGHEST = lax.Precision.HIGHEST
MESH = pl.DeviceIdType.MESH
F32, BF16 = jnp.float32, jnp.bfloat16
LANES = 128
HALO = 8
TRANSFERS = 224
GROUPS = 4


def dot(a, b, dims=((1,), (0,)), precision=None):
    return lax.dot_general(
        a, b, (dims, ((), ())), precision=precision, preferred_element_type=F32
    )


def dot2(a, b, dims=((1,), (0,))):
    high = a.astype(BF16)
    low = (a - high.astype(F32)).astype(BF16)
    return dot(high, b, dims) + dot(low, b, dims)


NT = ((1,), (1,))
TN = ((0,), (0,))


def flip(index, mask):
    bit = 1
    while bit <= mask:
        if mask & bit:
            index = index + bit - 2 * bit * ((index // bit) % 2)
        bit *= 2
    return index


def tile(i, width):
    return pl.ds(pl.multiple_of(i * width, width), width)


def loop(count, step):
    def run(i, carry):
        step(i)
        return carry

    lax.fori_loop(0, count, run, 0)


def when(condition, action):
    if condition is None:
        action()
    else:
        pl.when(condition)(action)


def sigmoid(v):
    return 1.0 / (1.0 + jnp.exp(-v))


class Transfer:
    def __init__(self, links, src, dst, to):
        self.links, self.src, self.dst, self.to = links, src, dst, to
        self.at = links.used
        links.used += 1
        assert links.used <= TRANSFERS

    def make(self):
        return pltpu.make_async_remote_copy(
            src_ref=self.src(),
            dst_ref=self.dst(),
            send_sem=self.links.send.at[self.at],
            recv_sem=self.links.recv.at[self.at],
            device_id=self.to,
            device_id_type=MESH,
        )

    def start(self, condition=None):
        when(condition, lambda: self.make().start())
        self.links.open.append((condition, self))

    def arrived(self, condition=None):
        when(condition, lambda: self.make().wait_recv())


class Links:
    def __init__(self, send, recv):
        self.send, self.recv, self.used, self.open = send, recv, 0, []

    def transfer(self, src, dst, to):
        return Transfer(self, src, dst, to)

    def close(self):
        for condition, item in self.open:
            when(condition, lambda item=item: item.make().wait_send())
        self.open = []


class Place:
    def __init__(self, seq, owners):
        self.s = lax.axis_index("section")
        self.f = lax.axis_index("fsdp")
        self.z = lax.axis_index("seq")
        self.nz = seq
        self.bits = [1 << k for k in range(owners.bit_length() - 1)]
        self.other = {"section": 1 - self.s}
        self.after = {"seq": lax.rem(self.z + 1, self.nz)}
        self.before = {"seq": lax.rem(self.z + self.nz - 1, self.nz)}
        self.first = self.z == 0
        self.last = self.z == self.nz - 1
        self.not_first = self.z > 0
        self.not_last = self.z < self.nz - 1

    def owner(self, mask):
        return flip(self.f, mask)

    def to_owner(self, mask):
        return {"fsdp": self.owner(mask)}


class Gather:
    def __init__(self, links, here, own, whole, rows, local_sem):
        self.here = here
        half = rows // 2

        def place(mask, part, count):
            start = here.owner(mask) * rows + part * half
            return whole.at[here.s, pl.ds(pl.multiple_of(start, half), count), :]

        self.local = lambda: pltpu.make_async_copy(own, place(0, 0, rows), local_sem)
        self.core = [
            links.transfer(lambda: own, lambda: place(0, 0, rows), here.other)
        ]
        self.phases = [[] for _ in here.bits]
        for part, order in enumerate((here.bits, here.bits[::-1])):
            known = [0]
            for k, bit in enumerate(order):
                for mask in known:
                    src = (
                        (lambda part=part: own.at[pl.ds(part * half, half), :])
                        if mask == 0
                        else (lambda mask=mask, part=part: place(mask, part, half))
                    )
                    item = links.transfer(
                        src,
                        lambda mask=mask, part=part: place(mask, part, half),
                        here.to_owner(bit),
                    )
                    got = lambda mask=mask, part=part, bit=bit: place(mask ^ bit, part, half)
                    core = links.transfer(got, got, here.other)
                    self.core.append(core)
                    self.phases[k].append((item, core))
                known = known + [mask ^ bit for mask in known]

    def start(self, condition):
        when(condition, lambda: self.local().start())
        for item, _ in self.phases[0]:
            item.start(condition)
        self.core[0].start(condition)

    def advance(self, k, condition):
        for item, _ in self.phases[k]:
            item.arrived(condition)
        if k + 1 < len(self.phases):
            for item, _ in self.phases[k + 1]:
                item.start(condition)
        for _, core in self.phases[k]:
            core.start(condition)

    def settle(self, condition):
        when(condition, lambda: self.local().wait())

    def from_other(self, condition):
        for core in self.core:
            core.arrived(condition)


class Fold:
    def __init__(self, links, here, own, mine, inward, total_in, total):
        z, half = here.z, here.nz // 2
        low = z < half
        self.ends = (z == 0) | (z == here.nz - 1)
        self.inner = jnp.logical_not(self.ends)
        self.middle = (z == half - 1) | (z == half)
        self.outer = jnp.logical_not(self.middle)
        into = {"seq": lax.rem(jnp.where(low, z + 1, z + here.nz - 1), here.nz)}
        out = {"seq": lax.rem(jnp.where(low, z + here.nz - 1, z + 1), here.nz)}
        self.own, self.inward, self.total_in, self.total = own, inward, total_in, total
        self.up = links.transfer(lambda: mine, lambda: inward, into)
        self.across = links.transfer(lambda: mine, lambda: total_in, into)
        self.down = links.transfer(lambda: total, lambda: total_in, out)
        self.mine = mine

    def start(self, add, put):
        def end():
            put(self.mine, None)

        def inner():
            self.up.arrived()
            put(self.mine, self.inward)

        when(self.ends, end)
        when(self.inner, inner)
        self.up.start(self.outer)
        self.across.start(self.middle)

    def finish(self, both, copy):
        def middle():
            self.across.arrived()
            both(self.total, self.mine, self.total_in)

        def outer():
            self.down.arrived()
            copy(self.total, self.total_in)

        when(self.middle, middle)
        when(self.outer, outer)
        self.down.start(self.inner)


def make_body(dims, names):
    T, D, PROJ, DI, HEADS, OWNERS = (
        dims.T, dims.D, dims.PROJ, dims.DI, dims.HEADS, dims.OWNERS,
    )
    LAYERS = 2
    DC = PROJ - DI
    N = (DC - DI) // 2
    HD = DI // HEADS
    EW, LW, OW = DI // 2, DC // 2, D // 2
    OA = (OW // LANES * 2 // 3) * LANES
    OB = OW - OA
    GW = DI // GROUPS
    PAIRS = DI // (2 * HD)
    PG = PAIRS // GROUPS
    RI, RO = D // OWNERS, DI // OWNERS
    EA = (EW // LANES // 2) * LANES
    LA = (LW // LANES // 2) * LANES
    SIZES = ((RI, EA), (RI, EW - EA), (RI, LA), (RI, LW - LA), (RO, OA), (RO, OB))
    E_A, E_B, L_A, L_B, OUT_A, OUT_B = range(6)
    NORM, TAPS, BIAS, SKIP, GATE = 0, 1, 5, 6, 7
    assert N == LANES and 2 * HD == LANES and T == LANES and dims.seq % 2 == 0

    scratch = dict(
        W=((LAYERS, D, PROJ), BF16),
        V=((LAYERS, DI, D), BF16),
        step=((LAYERS, HEADS, T), jnp.int32),
        decay=((LAYERS, HEADS, T), jnp.int32),
        params=((LAYERS, 8, DC), F32),
        small_in=((dims.NBITS, 8, DC), F32),
        small_mine=((dims.NBITS, 8, DC), F32),
        Dm=((LAYERS, PAIRS, T, 2 * T), F32),
        ecum=((LAYERS, T, DI), F32),
        toend=((LAYERS, T, DI), F32),
        hid=((LAYERS + 1, T, D), F32),
        cot=((LAYERS + 1, T, D), F32),
        nrm=((LAYERS, 2 * T, D), BF16),
        no=((LAYERS, 2 * T, DI), BF16),
        cb2=((LAYERS, 2 * T, OW), BF16),
        dE=((LAYERS, 2 * T, EW), BF16),
        dL=((LAYERS, 2 * T, LW), BF16),
        ext=((LAYERS, HALO + T, DC), F32),
        dpx=((T + HALO, DC), F32),
        dpx_out=((LAYERS, HALO, DC), F32),
        dpx_in=((LAYERS, HALO, DC), F32),
        gate=((LAYERS, T, DI), F32),
        act=((LAYERS, T, DC), F32),
        score=((LAYERS, T, T), F32),
        st=((LAYERS, N, DI), BF16),
        so=((LAYERS, N, DI), BF16),
        lv=((LAYERS, N, DI), BF16),
        part=((N, DI), F32),
        mixed=((LAYERS, T, DI), F32),
        r2=((LAYERS, T, 1), F32),
        cbf=((LAYERS, T, D), BF16),
        dno=((T, DI), F32),
        ed=((T, DI), F32),
        dproj=((LAYERS, T, PROJ), BF16),
        dact=((T, DC), F32),
        dsc=((T, T), F32),
        dB=((T, N), F32),
        dCq=((T, N), F32),
        dnr=((T, D), F32),
        sums=((2 * 8, DC), F32),
        sums_core=((2 * 8, DC), F32),
        sums_mine=((dims.NBITS + 1, 2 * 8, DC), F32),
        sums_in=((dims.NBITS, 2 * 8, DC), F32),
        sums_up=((2 * 8, DC), F32),
        sums_tin=((2 * 8, DC), F32),
        sums_total=((2 * 8, DC), F32),
    )
    sums = (
        [((LAYERS, OWNERS * rows, cols), BF16) for rows, cols in SIZES],
        [((LAYERS, OWNERS - 1, rows, cols), BF16) for rows, cols in SIZES],
        [((LAYERS, rows, cols), BF16) for rows, cols in SIZES],
        [((LAYERS, rows, cols), BF16) for rows, cols in SIZES],
    )

    def kernel(*refs):
        refs = list(refs)
        R = types.SimpleNamespace(**dict(zip(names, refs)))
        refs = refs[len(names) :]
        R.o_res, R.o_grad, R.o_in, R.o_out, R.o_small = refs[:5]
        refs = refs[5:]
        vars(R).update(zip(scratch, refs))
        refs = refs[len(scratch) :]
        R.g, R.rx, R.up, R.tin = [refs[6 * i : 6 * i + 6] for i in range(4)]
        sem_send, sem_recv, local = refs[24:]
        here = Place(dims.seq, OWNERS)
        links = Links(sem_send, sem_recv)
        s, f, z = here.s, here.f, here.z
        mine_rows = pl.ds(pl.multiple_of(s * T, T), T)
        W, V = R.W, R.V

        barrier = pltpu.get_barrier_semaphore()

        def greet(device, condition=None):
            when(
                condition,
                lambda: pl.semaphore_signal(barrier, inc=1, device_id=device, device_id_type=MESH),
            )

        greet(here.other)
        for bit in here.bits:
            greet(here.to_owner(bit))
        greet(here.after, here.not_last)
        greet(here.before, here.not_first)
        seq_partners = jnp.where(here.first, 0, 1) + jnp.where(here.last, 0, 1)
        pl.semaphore_wait(barrier, 1 + len(here.bits) + seq_partners)

        gather_in = Gather(links, here, R.input_weight.at[0], W, RI, local.at[0])
        gather_out = Gather(links, here, R.out_weight.at[0], V, RO, local.at[1])
        core0, core1 = s == 0, s == 1
        gather_in.start(core0)

        code_sends = []
        code_locals = []
        for at, key in enumerate(((R.step_codes, R.step), (R.decay_codes, R.decay))):
            ref, held = key
            item = links.transfer(
                lambda ref=ref: ref.at[0, 1 - s, 0], lambda held=held: held.at[s], here.other
            )
            item.start()
            code_sends.append(item)
            copy = pltpu.make_async_copy(ref.at[0, s, 0], held.at[s], local.at[2 + at])
            copy.start()
            code_locals.append(copy)
        hid_copy = pltpu.make_async_copy(R.inputs.at[s, 0], R.hid.at[0], local.at[4])
        hid_copy.start()
        cot_copy = pltpu.make_async_copy(R.out_grad.at[s, 0], R.cot.at[LAYERS], local.at[5])
        cot_copy.start()

        small = R.small_mine
        small[0] = jnp.zeros((8, DC), F32)
        wn, wc, wk, wg = D // OWNERS, DC // OWNERS, HEADS // OWNERS, DI // OWNERS
        small[0, 0:1, 0:wn] = R.norm_gain[...].astype(F32)
        small[0, 1:5, 0:wc] = R.conv_weight[0].astype(F32)
        small[0, 5:6, 0:wc] = R.conv_bias[...].astype(F32)
        skip = R.skip_gain[...].astype(F32)
        for head in range(wk):
            small[0, 6:7, head * HD : (head + 1) * HD] = jnp.broadcast_to(
                skip[:, head : head + 1], (1, HD)
            )
        small[0, 7:8, 0:wg] = R.gate_gain[...].astype(F32)
        raw = small[0]
        row = lax.broadcasted_iota(jnp.int32, (8, DC), 0)

        def turned(value, width, back):
            return pltpu.roll(value, lax.rem((DC - f * width if back else f * width), DC), 1)

        def by_row(value, back):
            out = turned(value, wc, back)
            out = jnp.where(row == 0, turned(value, wn, back), out)
            return jnp.where(row >= 6, turned(value, wg, back), out)

        small[0] = by_row(raw, False)
        small_steps = []
        for k, bit in enumerate(here.bits):
            item = links.transfer(
                lambda k=k: small.at[k], lambda k=k: R.small_in.at[k], here.to_owner(bit)
            )
            small_steps.append(item)
        small_core = links.transfer(
            lambda: R.params.at[s], lambda: R.params.at[s], here.other
        )
        small_steps[0].start()

        for copy in code_locals:
            copy.wait()
        for item in code_sends:
            item.arrived()
        lane = lax.broadcasted_iota(jnp.int32, (T, T), 1)
        sub = lax.broadcasted_iota(jnp.int32, (T, T), 0)
        causal = sub >= lane
        tri = jnp.where(causal, 1.0, 0.0).astype(F32)
        eye = jnp.where(sub == lane, 1.0, 0.0).astype(F32)
        spread = jnp.where(
            lax.broadcasted_iota(jnp.int32, (HEADS, DI), 1) // HD
            == lax.broadcasted_iota(jnp.int32, (HEADS, DI), 0),
            1.0,
            0.0,
        ).astype(F32)

        def prepare(layer):
            step_t = R.step[layer].astype(F32) / STEP_SCALE
            fall = R.decay[layer].astype(F32)
            cum = dot(tri, fall, NT, HIGHEST) / -DECAY_SCALE
            cum_t = dot(fall, tri, NT, HIGHEST) / -DECAY_SCALE
            steps = dot(eye, step_t, NT, HIGHEST)
            last = cum[T - 1 : T, :]
            R.ecum[layer] = dot(jnp.exp(cum), spread, precision=HIGHEST)
            R.toend[layer] = dot(jnp.exp(last - cum) * steps, spread, precision=HIGHEST)
            for head in range(HEADS):
                gap = cum[:, head : head + 1] - cum_t[head : head + 1, :]
                decays = jnp.where(causal, jnp.exp(jnp.where(causal, gap, 0.0)), 0.0)
                side = (head % 2) * T
                R.Dm[layer, head // 2, :, side : side + T] = decays * step_t[head : head + 1, :]

        prepare(0)
        gather_in.advance(0, core0)
        prepare(1)

        for k, item in enumerate(small_steps):
            item.arrived()
            total = small[k] + R.small_in[k]
            if k + 1 < len(small_steps):
                small[k + 1] = total
                small_steps[k + 1].start()
            else:
                R.params[s] = total
        small_core.start()
        small_core.arrived()
        hid_copy.wait()

        for k in range(1, len(here.bits)):
            gather_in.advance(k, core0)
        gather_out.start(core0)
        gather_in.settle(core0)
        gather_in.from_other(core1)
        gather_in.start(core1)

        low_lane = lane < HD

        def block_diag(pair):
            zero = jnp.zeros_like(pair)
            return jnp.concatenate(
                [jnp.where(low_lane, pair, zero), jnp.where(low_lane, zero, pair)], axis=0
            )

        def param(layer, name, cols, at=0):
            first = name + at
            return R.params[layer, first : first + 1, cols]

        def conv_argument(layer, cols):
            total = param(layer, BIAS, cols)
            for k in range(4):
                total = total + param(layer, TAPS, cols, k) * R.ext[
                    layer, HALO - 3 + k : HALO - 3 + k + T, cols
                ]
            return total

        def queries(layer):
            return R.act[layer, :, DI + N : DI + 2 * N]

        def input_keys(layer):
            return R.act[layer, :, DI : DI + N]

        share = [None] * LAYERS
        states = [None] * LAYERS

        def own_or_other(layer, src, out):
            item = links.transfer(lambda: src, lambda: out.at[0, s, 0], here.other)
            copy = lambda: pltpu.make_async_copy(src, out.at[0, s, 0], local.at[6])
            owner, guest = s == layer, s != layer
            when(owner, lambda: copy().start())
            item.start(guest)

            def end():
                when(owner, lambda: copy().wait())
                item.arrived(owner)

            return end

        def forward(layer, pump):
            hid = R.hid
            u = hid[layer]
            inverse = lax.rsqrt(jnp.mean(u * u, axis=1, keepdims=True) + EPSILON)
            R.nrm[layer, mine_rows, :] = (
                u * inverse * param(layer, NORM, slice(0, D))
            ).astype(BF16)
            swap_nrm = links.transfer(
                lambda: R.nrm.at[layer, mine_rows, :],
                lambda: R.nrm.at[layer, mine_rows, :],
                here.other,
            )
            swap_nrm.start()

            def project(i):
                normed = R.nrm[layer, mine_rows, :]
                R.ext[layer, HALO : HALO + T, tile(i, 256)] = dot(
                    normed, W[layer, :, pl.ds(pl.multiple_of(DI + i * 256, 256), 256)]
                )

            loop(DC // 256, project)
            halo = links.transfer(
                lambda: R.ext.at[layer, T : T + HALO, :],
                lambda: R.ext.at[layer, 0:HALO, :],
                here.after,
            )
            halo.start(here.not_last)

            def clear():
                R.ext[layer, 0:HALO, :] = jnp.zeros((HALO, DC), F32)
                R.st[layer] = jnp.zeros((N, DI), BF16)

            when(here.first, clear)

            def gates(i):
                normed = R.nrm[layer, mine_rows, :]
                R.gate[layer, :, tile(i, 256)] = dot(normed, W[layer, :, tile(i, 256)])

            loop(DI // 256, gates)
            halo.arrived(here.not_first)

            def convolve(i):
                v = conv_argument(layer, tile(i, LANES))
                R.act[layer, :, tile(i, LANES)] = v * sigmoid(v)

            loop(DC // LANES, convolve)
            pump(0)
            C, B = queries(layer), input_keys(layer)
            scores = dot(C, B, NT, HIGHEST)
            R.score[layer] = scores

            hand = []
            for g in range(GROUPS):
                cols = slice(g * GW, (g + 1) * GW)
                weighted = (R.act[layer, :, cols] * R.toend[layer, :, cols]).astype(BF16)
                R.part[:, cols] = dot2(B, weighted, TN)
                hand.append(
                    links.transfer(
                        lambda cols=cols: R.so.at[layer, :, cols],
                        lambda cols=cols: R.st.at[layer, :, cols],
                        here.after,
                    )
                )

            def first_sends():
                R.so[layer] = R.part[...].astype(BF16)
                for item in hand:
                    item.make().start()

            when(here.first, first_sends)
            for g in range(GROUPS):
                for pair in range(g * PG, (g + 1) * PG):
                    cols = slice(pair * LANES, (pair + 1) * LANES)
                    dm = R.Dm[layer, pair]
                    both = jnp.concatenate([dm[:, :T] * scores, dm[:, T:] * scores], axis=1)
                    x = R.act[layer, :, cols]
                    R.mixed[layer, :, cols] = (
                        dot(both.astype(BF16), block_diag(x.astype(BF16)))
                        + param(layer, SKIP, cols) * x
                    )
                cols = slice(g * GW, (g + 1) * GW)

                def pass_on(g=g, cols=cols):
                    hand[g].make().wait_recv()
                    R.so[layer, :, cols] = (
                        R.part[:, cols]
                        + R.ecum[layer, T - 1 : T, cols] * R.st[layer, :, cols].astype(F32)
                    ).astype(BF16)

                when(here.not_first, pass_on)
                when(here.not_first & here.not_last, lambda g=g: hand[g].make().start())
                R.mixed[layer, :, cols] += R.ecum[layer, :, cols] * dot2(
                    C, R.st[layer, :, cols]
                )

            pump(1)

            def gating(i, squares):
                cols = tile(i, LANES)
                gate = R.gate[layer, :, cols]
                value = R.mixed[layer, :, cols] * (gate * sigmoid(gate))
                return squares + value * value

            squares = lax.fori_loop(0, DI // LANES, gating, jnp.zeros((T, LANES), F32))
            r2 = lax.rsqrt(jnp.sum(squares, axis=1, keepdims=True) / DI + EPSILON)
            R.r2[layer] = r2

            def scaled(i):
                cols = tile(i, LANES)
                gate = R.gate[layer, :, cols]
                value = R.mixed[layer, :, cols] * (gate * sigmoid(gate))
                R.no[layer, mine_rows, cols] = (
                    value * r2 * param(layer, GATE, cols)
                ).astype(BF16)

            loop(DI // LANES, scaled)
            swap_no = links.transfer(
                lambda: R.no.at[layer, mine_rows, :],
                lambda: R.no.at[layer, mine_rows, :],
                here.other,
            )
            swap_no.start()
            pump(2)

            def output(i):
                hid[layer + 1, :, tile(i, 256)] = hid[layer, :, tile(i, 256)] + dot(
                    R.no[layer, mine_rows, :], V[layer, :, tile(i, 256)]
                )

            loop(D // 256, output)
            share[layer] = types.SimpleNamespace(nrm=swap_nrm, no=swap_no)
            states[layer] = hand
            return own_or_other(layer, hid.at[layer + 1], R.o_res)

        deep = range(1, len(here.bits))

        def during_0(point):
            if point == 0:
                gather_out.advance(0, core0)
            elif point == 1:
                gather_in.advance(0, core1)
            else:
                for k in deep:
                    gather_out.advance(k, core0)
                gather_out.settle(core0)
                gather_out.from_other(core1)

        def during_1(point):
            if point == 1:
                gather_out.advance(0, core1)
            elif point == 2:
                for k in deep:
                    gather_out.advance(k, core1)
                gather_out.settle(core1)
                gather_out.from_other(core0)

        ends = [forward(0, during_0)]
        for k in deep:
            gather_in.advance(k, core1)
        gather_out.start(core1)
        gather_in.settle(core1)
        gather_in.from_other(core0)
        ends.append(forward(1, during_1))
        for end in ends:
            end()
        cot_copy.wait()

        def add_row(layer, name, cols, value, at=0):
            first = 8 * layer + name + at
            R.sums[first : first + 1, cols] = jnp.sum(value, axis=0, keepdims=True)

        def half_swap(layer, src, dst, width):
            item = links.transfer(
                lambda: src.at[:, pl.ds(pl.multiple_of((1 - s) * width, LANES), width)],
                lambda: dst.at[layer, mine_rows, :],
                here.other,
            )
            item.start()
            dst[layer, mine_rows, :] = src[:, pl.ds(pl.multiple_of(s * width, LANES), width)]
            return item

        R.sums[...] = jnp.zeros((2 * 8, DC), F32)

        def backward(layer, plan):
            plan = iter(plan)

            def pump():
                for action in next(plan):
                    action()

            hid, cot = R.hid, R.cot
            R.cbf[layer] = cot[layer + 1].astype(BF16)
            share[layer].cb = half_swap(layer, R.cbf.at[layer], R.cb2, OW)
            r2 = R.r2[layer]

            def first_pass(i, total):
                cols = tile(i, 256)
                d = dot(R.cbf[layer], V[layer, cols, :], NT)
                R.dno[:, cols] = d
                gate = R.gate[layer, :, cols]
                gated = R.mixed[layer, :, cols] * (gate * sigmoid(gate))
                add_row(layer, GATE, cols, d * gated * r2)
                return total + jnp.sum(
                    d * param(layer, GATE, cols) * gated, axis=1, keepdims=True
                )

            total = lax.fori_loop(0, DI // 256, first_pass, jnp.zeros((T, 1), F32))
            factor = r2 * r2 * r2 * total / DI
            pump()
            dproj = R.dproj.at[layer]

            def second_pass(i):
                cols = tile(i, LANES)
                gate = R.gate[layer, :, cols]
                sg = sigmoid(gate)
                dg = (
                    R.dno[:, cols] * param(layer, GATE, cols) * r2
                    - R.mixed[layer, :, cols] * (gate * sg) * factor
                )
                dm = dg * (gate * sg)
                R.dno[:, cols] = dm
                dproj[:, cols] = (
                    dg * R.mixed[layer, :, cols] * (sg * (1.0 + gate * (1.0 - sg)))
                ).astype(BF16)
                R.ed[:, cols] = dm * R.ecum[layer, :, cols]
                add_row(layer, SKIP, cols, dm * R.act[layer, :, cols])

            loop(DI // LANES, second_pass)
            share[layer].e = half_swap(layer, dproj, R.dE, EW)
            pump()
            C, B = queries(layer), input_keys(layer)
            for item in states[layer]:
                when(here.not_last, lambda item=item: item.make().wait_send())
            hand = []
            for g in range(GROUPS):
                cols = slice(g * GW, (g + 1) * GW)
                R.part[:, cols] = dot2(C, R.ed[:, cols].astype(BF16), TN)
                hand.append(
                    links.transfer(
                        lambda cols=cols: R.so.at[layer, :, cols],
                        lambda cols=cols: R.lv.at[layer, :, cols],
                        here.before,
                    )
                )

            def first_sends():
                R.lv[layer] = jnp.zeros((N, DI), BF16)
                R.dpx_in[layer] = jnp.zeros((HALO, DC), F32)
                R.so[layer] = R.part[...].astype(BF16)
                for item in hand:
                    item.make().start()

            when(here.last, first_sends)
            scores = R.score[layer]
            R.dsc[...] = jnp.zeros((T, T), F32)
            R.dB[...] = jnp.zeros((T, N), F32)
            R.dCq[...] = jnp.zeros((T, N), F32)
            for g in range(GROUPS):
                for pair in range(g * PG, (g + 1) * PG):
                    cols = slice(pair * LANES, (pair + 1) * LANES)
                    dm = R.dno[:, cols]
                    dmb = dm.astype(BF16)
                    decays = R.Dm[layer, pair]
                    x = R.act[layer, :, cols].astype(BF16)
                    dc = dot(dmb, block_diag(x), NT)
                    R.dsc[...] += decays[:, :T] * dc[:, :T] + decays[:, T:] * dc[:, T:]
                    both = jnp.concatenate([decays[:, :T] * scores, decays[:, T:] * scores], axis=1)
                    back = dot(both.astype(BF16), dmb, TN)
                    R.dact[:, cols] = param(layer, SKIP, cols) * dm + jnp.where(
                        low_lane, back[:T], back[T:]
                    )
                cols = slice(g * GW, (g + 1) * GW)

                def pass_on(g=g, cols=cols):
                    hand[g].make().wait_recv()
                    R.so[layer, :, cols] = (
                        R.part[:, cols]
                        + R.ecum[layer, T - 1 : T, cols] * R.lv[layer, :, cols].astype(F32)
                    ).astype(BF16)

                when(here.not_last, pass_on)
                when(here.not_first & here.not_last, lambda g=g: hand[g].make().start())
                links.open.append((here.not_first, hand[g]))
                leaving = R.lv[layer, :, cols]
                toend = R.toend[layer, :, cols]
                R.dact[:, cols] += toend * dot2(B, leaving)
                R.dB[...] += dot2(R.act[layer, :, cols] * toend, leaving, NT)
                R.dCq[...] += dot2(R.ed[:, cols], R.st[layer, :, cols], NT)
                pump()
            dsc = R.dsc[...]
            R.dact[:, DI : DI + N] = R.dB[...] + dot(dsc, C, TN, HIGHEST)
            R.dact[:, DI + N :] = R.dCq[...] + dot(dsc, B, precision=HIGHEST)

            def conv_back(i):
                cols = tile(i, LANES)
                v = conv_argument(layer, cols)
                sg = sigmoid(v)
                d = R.dact[:, cols] * (sg * (1.0 + v * (1.0 - sg)))
                R.dpx[0:T, cols] = d
                R.dpx_out[layer, :, cols] = d[:HALO]
                add_row(layer, BIAS, cols, d)
                for k in range(4):
                    add_row(
                        layer,
                        TAPS,
                        cols,
                        d * R.ext[layer, HALO - 3 + k : HALO - 3 + k + T, cols],
                        k,
                    )

            loop(DC // LANES, conv_back)
            halo = links.transfer(
                lambda: R.dpx_out.at[layer],
                lambda: R.dpx_in.at[layer],
                here.before,
            )
            halo.start(here.not_first)
            pump()
            halo.arrived(here.not_last)
            R.dpx[T : T + HALO, :] = R.dpx_in[layer]

            def rows_back(i):
                cols = tile(i, LANES)
                total = param(layer, TAPS, cols, 3) * R.dpx[0:T, cols]
                for k in range(3):
                    total = total + param(layer, TAPS, cols, k) * R.dpx[
                        3 - k : 3 - k + T, cols
                    ]
                dproj[:, pl.ds(pl.multiple_of(DI + i * LANES, LANES), LANES)] = total.astype(BF16)

            loop(DC // LANES, rows_back)
            share[layer].l = half_swap(layer, R.dproj.at[layer, :, pl.ds(DI, DC)], R.dL, LW)
            pump()

            def normed_back(i):
                R.dnr[:, tile(i, 256)] = dot(dproj[...], W[layer, tile(i, 256), :], NT)

            loop(D // 256, normed_back)
            pump()
            u = hid[layer]
            inverse = lax.rsqrt(jnp.mean(u * u, axis=1, keepdims=True) + EPSILON)
            dn = R.dnr[...]
            add_row(layer, NORM, slice(0, D), dn * u * inverse)
            da = dn * param(layer, NORM, slice(0, D))
            pull = jnp.sum(da * u, axis=1, keepdims=True)
            cot[layer] = (
                cot[layer + 1] + da * inverse - u * (inverse * inverse * inverse * pull / D)
            )
            return own_or_other(layer, cot.at[layer], R.o_grad)

        def out_grads(layer):
            share[layer].no.arrived()
            share[layer].cb.arrived()

            def part(i):
                value = dot(R.no[layer, :, tile(i, 256)], R.cb2[layer], TN).astype(BF16)
                R.g[OUT_A][layer, tile(i, 256), :] = value[:, :OA]
                R.g[OUT_B][layer, tile(i, 256), :] = value[:, OA:]

            loop(DI // 256, part)

        def in_grads(layer, came, right, a, b):
            came.arrived()

            def part(i):
                value = dot(R.nrm[layer, :, tile(i, 256)], right[layer], TN).astype(BF16)
                split = R.g[a].shape[-1]
                R.g[a][layer, tile(i, 256), :] = value[:, :split]
                R.g[b][layer, tile(i, 256), :] = value[:, split:]

            loop(D // 256, part)

        def gate_grads(layer):
            share[layer].nrm.arrived()
            in_grads(layer, share[layer].e, R.dE, E_A, E_B)

        def row_grads(layer):
            in_grads(layer, share[layer].l, R.dL, L_A, L_B)

        class Reduce:
            def __init__(self, layer, key, order, cols, out):
                self.layer, self.order = layer, order
                rows, width = SIZES[key]
                self.rows = rows
                self.g = R.g[key].at[layer]
                rx = R.rx[key].at[layer]
                self.phases = []
                slot = 0
                for k, bit in enumerate(order):
                    masks = [0]
                    for rest in order[k + 1 :]:
                        masks = masks + [m ^ rest for m in masks]
                    phase = []
                    for mask in masks:
                        item = links.transfer(
                            lambda bit=bit, mask=mask: self.g.at[self.block(bit ^ mask), :],
                            lambda slot=slot: rx.at[slot],
                            here.to_owner(bit),
                        )
                        phase.append((item, mask, rx.at[slot]))
                        slot += 1
                    self.phases.append(phase)
                self.fold = Fold(
                    links, here, None, self.g.at[self.block(0), :], R.up[key].at[layer],
                    R.tin[key].at[layer], rx.at[slot - 1],
                )
                total = rx.at[slot - 1]
                place = lambda: out.at[
                    :, pl.ds(pl.multiple_of(cols[0] + s * cols[1], LANES), width)
                ]
                self.owner, self.guest = s == layer, s != layer
                self.out = links.transfer(lambda: total, place, here.other)
                sem = local.at[8 + 6 * layer + key]
                self.local = lambda: pltpu.make_async_copy(total, place(), sem)
                self.chunk = 32 if rows % 32 == 0 else 16

            def block(self, mask):
                return pl.ds(pl.multiple_of(here.owner(mask) * self.rows, self.rows), self.rows)

            def piece(self, i, start=0):
                return pl.ds(pl.multiple_of(start + i * self.chunk, self.chunk), self.chunk)

            def start(self):
                for item, _, _ in self.phases[0]:
                    item.start()

            def advance(self, k):
                for item, mask, got in self.phases[k]:
                    item.arrived()

                    def add(i, mask=mask, got=got):
                        at = self.piece(i, here.owner(mask) * self.rows)
                        self.g[at, :] = (
                            self.g[at, :].astype(F32) + got[self.piece(i), :].astype(F32)
                        ).astype(BF16)

                    loop(self.rows // self.chunk, add)
                for item, _, _ in self.phases[k + 1]:
                    item.start()

            def to_fold(self):
                (item, _, got), = self.phases[-1]
                item.arrived()

                def put(dst, extra):
                    def add(i):
                        value = self.g[self.piece(i, f * self.rows), :].astype(F32) + got[
                            self.piece(i), :
                        ].astype(F32)
                        if extra is not None:
                            value = value + extra[self.piece(i), :].astype(F32)
                        self.g[self.piece(i, f * self.rows), :] = value.astype(BF16)

                    loop(self.rows // self.chunk, add)

                self.fold.start(None, put)

            def finish(self):
                def both(dst, a, b):
                    def add(i):
                        dst[self.piece(i), :] = (
                            self.g[self.piece(i, f * self.rows), :].astype(F32) + b[self.piece(i), :].astype(F32)
                        ).astype(BF16)

                    loop(self.rows // self.chunk, add)

                def copy(dst, a):
                    def move(i):
                        dst[self.piece(i), :] = a[self.piece(i), :]

                    loop(self.rows // self.chunk, move)

                self.fold.finish(both, copy)
                when(self.owner, lambda: self.local().start())
                self.out.start(self.guest)

            def end(self):
                when(self.owner, lambda: self.local().wait())
                self.out.arrived(self.owner)

        class Both:
            def __init__(self, *items):
                self.items = items

            def start(self):
                for item in self.items:
                    item.start()

            def advance(self):
                for k in range(len(here.bits) - 1):
                    for item in self.items:
                        item.advance(k)

            def to_fold(self):
                for item in self.items:
                    item.to_fold()

            def finish(self):
                for item in self.items:
                    item.finish()

            def end(self):
                for item in self.items:
                    item.end()

        straight, backwards = here.bits, here.bits[::-1]
        out, gates_in, rows_in = [], [], []
        for layer in range(LAYERS):
            out.append(
                Both(
                    Reduce(layer, OUT_A, straight, (0, OW), R.o_out),
                    Reduce(layer, OUT_B, backwards, (OA, OW), R.o_out),
                )
            )
            gates_in.append(
                Both(
                    Reduce(layer, E_A, backwards, (0, EW), R.o_in),
                    Reduce(layer, E_B, straight, (EA, EW), R.o_in),
                )
            )
            rows_in.append(
                Both(
                    Reduce(layer, L_A, straight, (DI, LW), R.o_in),
                    Reduce(layer, L_B, backwards, (DI + LA, LW), R.o_in),
                )
            )

        plan1 = (
            [lambda: out_grads(1), out[1].start],
            [],
            [lambda: gate_grads(1), gates_in[1].start],
            [],
            [out[1].advance],
            [],
            [gates_in[1].advance],
            [out[1].to_fold],
            [],
        )
        plan0 = (
            [lambda: row_grads(1), rows_in[1].start],
            [lambda: out_grads(0), out[0].start, gates_in[1].to_fold],
            [out[1].finish],
            [lambda: gate_grads(0), gates_in[0].start],
            [rows_in[1].advance],
            [out[0].advance, gates_in[1].finish],
            [gates_in[0].advance, rows_in[1].to_fold],
            [lambda: row_grads(0), rows_in[0].start, out[0].to_fold],
            [gates_in[0].to_fold, rows_in[1].finish],
        )
        ends = [backward(1, plan1), backward(0, plan0)]

        sums_core = links.transfer(lambda: R.sums, lambda: R.sums_core, here.other)
        sums_core.start()
        sums_core.arrived()
        R.sums_mine[0] = R.sums[...] + R.sums_core[...]
        steps = [
            links.transfer(
                lambda k=k: R.sums_mine.at[k],
                lambda k=k: R.sums_in.at[k],
                here.to_owner(bit),
            )
            for k, bit in enumerate(here.bits)
        ]
        steps[0].start()
        out[0].finish()
        rows_in[0].advance()
        small_fold = Fold(
            links, here, None, R.sums_mine.at[len(here.bits)], R.sums_up, R.sums_tin,
            R.sums_total,
        )
        for k in range(len(here.bits) - 1):
            steps[k].arrived()
            R.sums_mine[k + 1] = R.sums_mine[k] + R.sums_in[k]
            steps[k + 1].start()
        gates_in[0].finish()
        rows_in[0].to_fold()
        k = len(here.bits) - 1
        steps[k].arrived()

        def put(dst, extra):
            value = R.sums_mine[k] + R.sums_in[k]
            dst[...] = value if extra is None else value + extra[...]

        small_fold.start(None, put)
        rows_in[0].finish()

        def both(dst, a, b):
            dst[...] = a[...] + b[...]

        def copy(dst, a):
            dst[...] = a[...]

        small_fold.finish(both, copy)
        total = R.sums_total[pl.ds(pl.multiple_of(s * 8, 8), 8), :]
        R.o_small[...] = by_row(total, True)[:, : R.o_small.shape[1]]
        for item in out + gates_in + rows_in:
            item.end()
        for end in ends:
            end()
        links.close()

    return kernel, list(scratch.values()) + sum(sums, [])


def body(
    inputs,
    out_grad,
    norm_gain,
    input_weight,
    conv_weight,
    conv_bias,
    skip_gain,
    gate_gain,
    out_weight,
    step_codes,
    decay_codes,
):
    given = types.SimpleNamespace(**locals())
    names = tuple(vars(given))
    owners, seq = lax.axis_size("fsdp"), lax.axis_size("seq")
    assert lax.axis_size("section") == 2 and owners & (owners - 1) == 0 and owners > 1
    T, D = given.inputs.shape[2:]
    rows_in, PROJ = given.input_weight.shape[1:]
    rows_out = given.out_weight.shape[1]
    DI = rows_out * owners
    HEADS = given.step_codes.shape[-1]
    given.step_codes = jnp.swapaxes(step_codes, -1, -2)
    given.decay_codes = jnp.swapaxes(decay_codes, -1, -2)
    arrays = tuple(vars(given).values())
    dims = types.SimpleNamespace(
        T=T, D=D, PROJ=PROJ, DI=DI, HEADS=HEADS, OWNERS=owners, seq=seq,
        NBITS=owners.bit_length() - 1,
    )
    kernel, scratch = make_body(dims, names)
    vmem = pl.BlockSpec(memory_space=pltpu.VMEM)
    hbm = pl.BlockSpec(memory_space=pl.ANY)
    small_width = -(-(PROJ - DI) // owners // LANES) * LANES
    part = (1, given.inputs.shape[0], 1, T, D)
    out_shape = (
        jax.ShapeDtypeStruct(part, F32),
        jax.ShapeDtypeStruct(part, F32),
        jax.ShapeDtypeStruct((rows_in, PROJ), BF16),
        jax.ShapeDtypeStruct((rows_out, D), BF16),
        jax.ShapeDtypeStruct((8, small_width), F32),
    )
    results, gradients, grad_in, grad_out, small = pl.pallas_call(
        kernel,
        out_shape=out_shape,
        in_specs=[hbm if array.ndim > 3 and array.dtype == F32 or array.size > 2**17 else vmem for array in arrays],
        out_specs=(hbm, hbm, hbm, hbm, vmem),
        scratch_shapes=[pltpu.VMEM(shape, dtype) for shape, dtype in scratch]
        + [
            pltpu.SemaphoreType.DMA((TRANSFERS,)),
            pltpu.SemaphoreType.DMA((TRANSFERS,)),
            pltpu.SemaphoreType.DMA((24,)),
        ],
        compiler_params=pltpu.CompilerParams(
            collective_id=0, has_side_effects=True, vmem_limit_bytes=63 * 2**20
        ),
    )(*arrays)
    wn, wc, wg = given.norm_gain.shape[1], given.conv_bias.shape[1], rows_out
    heads = given.skip_gain.shape[1]
    return (
        results,
        gradients,
        small[0:1, :wn],
        grad_in.astype(F32)[None],
        small[1:5, :wc][None],
        small[5:6, :wc],
        small[6, :wg].reshape(1, heads, -1).sum(axis=-1),
        small[7:8, :wg],
        grad_out.astype(F32)[None],
    )


def solution(mesh):
    return jax.shard_map(
        body,
        mesh=mesh,
        in_specs=(
            P(None, "fsdp", "seq", None),
            P(None, "fsdp", "seq", None),
            P("section", "fsdp"),
            P("section", "fsdp", None),
            P("section", None, "fsdp"),
            P("section", "fsdp"),
            P("section", "fsdp"),
            P("section", "fsdp"),
            P("section", "fsdp", None),
            P("section", None, "fsdp", "seq", None),
            P("section", None, "fsdp", "seq", None),
        ),
        out_specs=(
            P("section", None, "fsdp", "seq", None),
            P("section", None, "fsdp", "seq", None),
            P("section", "fsdp"),
            P("section", "fsdp", None),
            P("section", None, "fsdp"),
            P("section", "fsdp"),
            P("section", "fsdp"),
            P("section", "fsdp"),
            P("section", "fsdp", None),
        ),
        check_vma=False,
    )
```

```python
import types

import jax
import jax.numpy as jnp
from jax import lax
from jax.experimental import pallas as pl
from jax.experimental.pallas import tpu as pltpu
from jax.sharding import PartitionSpec as P

EPSILON = 1e-05
STEP_SCALE = 256.0
DECAY_SCALE = 65536.0
HIGHEST = lax.Precision.HIGHEST
MESH = pl.DeviceIdType.MESH
F32, BF16 = jnp.float32, jnp.bfloat16
LANES = 128
HALO = 8
TRANSFERS = 240
GROUPS = 6


def dot(a, b, dims=((1,), (0,)), precision=None):
    return lax.dot_general(
        a, b, (dims, ((), ())), precision=precision, preferred_element_type=F32
    )


def dot2(a, b, dims=((1,), (0,))):
    high = a.astype(BF16)
    low = (a - high.astype(F32)).astype(BF16)
    return dot(high, b, dims) + dot(low, b, dims)


NT = ((1,), (1,))
TN = ((0,), (0,))


def flip(index, mask):
    bit = 1
    while bit <= mask:
        if mask & bit:
            index = index + bit - 2 * bit * ((index // bit) % 2)
        bit *= 2
    return index


def tile(i, width):
    return pl.ds(pl.multiple_of(i * width, width), width)


def loop(count, step):
    def run(i, carry):
        step(i)
        return carry

    lax.fori_loop(0, count, run, 0)


def when(condition, action):
    if condition is None:
        action()
    else:
        pl.when(condition)(action)


def sigmoid(v):
    return 1.0 / (1.0 + jnp.exp(-v))


class Transfer:
    def __init__(self, links, src, dst, to):
        self.links, self.src, self.dst, self.to = links, src, dst, to
        self.at = links.used
        links.used += 1
        assert links.used <= TRANSFERS

    def make(self):
        return pltpu.make_async_remote_copy(
            src_ref=self.src(),
            dst_ref=self.dst(),
            send_sem=self.links.send.at[self.at],
            recv_sem=self.links.recv.at[self.at],
            device_id=self.to,
            device_id_type=MESH,
        )

    def start(self, condition=None):
        when(condition, lambda: self.make().start())
        self.links.open.append((condition, self))

    def arrived(self, condition=None):
        when(condition, lambda: self.make().wait_recv())


class Links:
    def __init__(self, send, recv):
        self.send, self.recv, self.used, self.open = send, recv, 0, []

    def transfer(self, src, dst, to):
        return Transfer(self, src, dst, to)

    def close(self):
        for condition, item in self.open:
            when(condition, lambda item=item: item.make().wait_send())
        self.open = []


class Place:
    def __init__(self, seq, owners):
        self.s = lax.axis_index("section")
        self.f = lax.axis_index("fsdp")
        self.z = lax.axis_index("seq")
        self.nz = seq
        self.bits = [1 << k for k in range(owners.bit_length() - 1)]
        self.other = {"section": 1 - self.s}
        self.after = {"seq": lax.rem(self.z + 1, self.nz)}
        self.before = {"seq": lax.rem(self.z + self.nz - 1, self.nz)}
        self.first = self.z == 0
        self.last = self.z == self.nz - 1
        self.not_first = self.z > 0
        self.not_last = self.z < self.nz - 1

    def owner(self, mask):
        return flip(self.f, mask)

    def to_owner(self, mask):
        return {"fsdp": self.owner(mask)}


class Gather:
    def __init__(self, links, here, own, whole, rows, cols, local_sem):
        self.here = here
        half = rows // 2

        def place(mask, part, count):
            start = here.owner(mask) * rows + part * half
            return whole.at[here.s, pl.ds(pl.multiple_of(start, half), count), cols]

        self.local = lambda: pltpu.make_async_copy(
            own.at[:, cols], place(0, 0, rows), local_sem
        )
        self.core = [
            links.transfer(lambda: own.at[:, cols], lambda: place(0, 0, rows), here.other)
        ]
        self.phases = [[] for _ in here.bits]
        for part, order in enumerate((here.bits, here.bits[::-1])):
            known = [0]
            for k, bit in enumerate(order):
                for mask in known:
                    src = (
                        (lambda part=part: own.at[pl.ds(part * half, half), cols])
                        if mask == 0
                        else (lambda mask=mask, part=part: place(mask, part, half))
                    )
                    item = links.transfer(
                        src,
                        lambda mask=mask, part=part: place(mask, part, half),
                        here.to_owner(bit),
                    )
                    got = lambda mask=mask, part=part, bit=bit: place(mask ^ bit, part, half)
                    core = links.transfer(got, got, here.other)
                    self.core.append(core)
                    self.phases[k].append((item, core, mask == 0))
                known = known + [mask ^ bit for mask in known]

    def start(self, condition):
        when(condition, lambda: self.local().start())
        self.core[0].start(condition)
        for phase in self.phases:
            for item, _, own in phase:
                if own:
                    item.start(condition)

    def advance(self, k, condition):
        for item, _, _ in self.phases[k]:
            item.arrived(condition)
        if k + 1 < len(self.phases):
            for item, _, own in self.phases[k + 1]:
                if not own:
                    item.start(condition)
        for _, core, _ in self.phases[k]:
            core.start(condition)

    def rest(self, condition):
        for k in range(1, len(self.phases)):
            self.advance(k, condition)
        when(condition, lambda: self.local().wait())

    def from_other(self, condition):
        for core in self.core:
            core.arrived(condition)


class Fold:
    def __init__(self, links, here, own, mine, inward, total_in, total):
        z, half = here.z, here.nz // 2
        low = z < half
        self.ends = (z == 0) | (z == here.nz - 1)
        self.inner = jnp.logical_not(self.ends)
        self.middle = (z == half - 1) | (z == half)
        self.outer = jnp.logical_not(self.middle)
        into = {"seq": lax.rem(jnp.where(low, z + 1, z + here.nz - 1), here.nz)}
        out = {"seq": lax.rem(jnp.where(low, z + here.nz - 1, z + 1), here.nz)}
        self.own, self.inward, self.total_in, self.total = own, inward, total_in, total
        self.up = links.transfer(lambda: mine, lambda: inward, into)
        self.across = links.transfer(lambda: mine, lambda: total_in, into)
        self.down = links.transfer(lambda: total, lambda: total_in, out)
        self.mine = mine

    def begin(self, put):
        when(self.ends, lambda: put(None))
        self.up.start(self.ends & self.outer)
        self.across.start(self.ends & self.middle)

    def collect(self, put):
        def inner():
            self.up.arrived()
            put(self.inward)

        when(self.inner, inner)
        self.up.start(self.inner & self.outer)
        self.across.start(self.inner & self.middle)

    def turn(self, both):
        def middle():
            self.across.arrived()
            both(self.total, self.mine, self.total_in)

        when(self.middle, middle)
        self.down.start(self.middle & self.inner)

    def settle(self, copy):
        def outer():
            self.down.arrived()
            copy(self.total, self.total_in)

        when(self.outer, outer)
        self.down.start(self.outer & self.inner)


def make_body(dims, names):
    T, D, PROJ, DI, HEADS, OWNERS = (
        dims.T, dims.D, dims.PROJ, dims.DI, dims.HEADS, dims.OWNERS,
    )
    LAYERS = 2
    DC = PROJ - DI
    N = (DC - DI) // 2
    HD = DI // HEADS
    EW, LW, OW = DI // 2, DC // 2, D // 2
    OA = (OW // LANES * 2 // 3) * LANES
    OB = OW - OA
    GW = DI // GROUPS
    PAIRS = DI // (2 * HD)
    PG = PAIRS // GROUPS
    RI, RO = D // OWNERS, DI // OWNERS
    EA = (EW // LANES // 2) * LANES
    LA = (LW // LANES // 2) * LANES
    SIZES = ((RI, EA), (RI, EW - EA), (RI, LA), (RI, LW - LA), (RO, OA), (RO, OB))
    E_A, E_B, L_A, L_B, OUT_A, OUT_B = range(6)
    NORM, TAPS, BIAS, SKIP, GATE = 0, 1, 5, 6, 7
    assert N == LANES and 2 * HD == LANES and T == LANES and dims.seq % 2 == 0

    scratch = dict(
        W=((LAYERS, D, PROJ), BF16),
        V=((LAYERS, DI, D), BF16),
        step=((LAYERS, HEADS, T), jnp.int32),
        decay=((LAYERS, HEADS, T), jnp.int32),
        params=((LAYERS, 8, DC), F32),
        small_in=((dims.NBITS, 8, DC), F32),
        small_mine=((dims.NBITS, 8, DC), F32),
        Dm=((LAYERS, PAIRS, T, 2 * T), F32),
        ecum=((LAYERS, T, DI), F32),
        toend=((LAYERS, T, DI), F32),
        hid=((LAYERS + 1, T, D), F32),
        cot=((LAYERS + 1, T, D), F32),
        nrm=((LAYERS, 2 * T, D), BF16),
        no=((LAYERS, 2 * T, DI), BF16),
        cb2=((LAYERS, 2 * T, OW), BF16),
        dE=((LAYERS, 2 * T, EW), BF16),
        dL=((LAYERS, 2 * T, LW), BF16),
        ext=((LAYERS, HALO + T, DC), F32),
        dpx=((T + HALO, DC), F32),
        dpx_out=((LAYERS, HALO, DC), F32),
        dpx_in=((LAYERS, HALO, DC), F32),
        gate=((LAYERS, T, DI), F32),
        act=((LAYERS, T, DC), F32),
        score=((LAYERS, T, T), F32),
        st=((LAYERS, N, DI), BF16),
        so=((LAYERS, N, DI), BF16),
        lv=((LAYERS, N, DI), BF16),
        part=((N, DI), F32),
        mixed=((LAYERS, T, DI), F32),
        r2=((LAYERS, T, 1), F32),
        cbf=((LAYERS, T, D), BF16),
        dno=((T, DI), F32),
        ed=((T, DI), F32),
        dproj=((LAYERS, T, PROJ), BF16),
        dact=((T, DC), F32),
        dsc=((T, T), F32),
        dB=((T, N), F32),
        dCq=((T, N), F32),
        dnr=((T, D), F32),
        sums=((2 * 8, DC), F32),
        sums_core=((8, DC), F32),
        sums_mine=((dims.NBITS + 1, 8, DC), F32),
        sums_in=((dims.NBITS, 8, DC), F32),
        sums_up=((8, DC), F32),
        sums_tin=((8, DC), F32),
        sums_total=((8, DC), F32),
    )
    sums = (
        [((LAYERS, OWNERS * rows, cols), BF16) for rows, cols in SIZES],
        [((LAYERS, OWNERS - 1, rows, cols), BF16) for rows, cols in SIZES],
        [((LAYERS, rows, cols), BF16) for rows, cols in SIZES],
        [((LAYERS, rows, cols), BF16) for rows, cols in SIZES],
    )

    def kernel(*refs):
        refs = list(refs)
        R = types.SimpleNamespace(**dict(zip(names, refs)))
        refs = refs[len(names) :]
        R.o_res, R.o_grad, R.o_in, R.o_out, R.o_small = refs[:5]
        refs = refs[5:]
        vars(R).update(zip(scratch, refs))
        refs = refs[len(scratch) :]
        R.g, R.rx, R.up, R.tin = [refs[6 * i : 6 * i + 6] for i in range(4)]
        sem_send, sem_recv, local = refs[24:]
        here = Place(dims.seq, OWNERS)
        links = Links(sem_send, sem_recv)
        s, f, z = here.s, here.f, here.z
        mine_rows = pl.ds(pl.multiple_of(s * T, T), T)
        W, V = R.W, R.V

        barrier = pltpu.get_barrier_semaphore()

        def greet(device, condition=None):
            when(
                condition,
                lambda: pl.semaphore_signal(barrier, inc=1, device_id=device, device_id_type=MESH),
            )

        greet(here.other)
        for bit in here.bits:
            greet(here.to_owner(bit))
        greet(here.after, here.not_last)
        greet(here.before, here.not_first)
        seq_partners = jnp.where(here.first, 0, 1) + jnp.where(here.last, 0, 1)
        pl.semaphore_wait(barrier, 1 + len(here.bits) + seq_partners)

        own_in = R.input_weight.at[0]
        gather_rows = Gather(links, here, own_in, W, RI, pl.ds(DI, DC), local.at[0])
        gather_gates = Gather(links, here, own_in, W, RI, pl.ds(0, DI), local.at[7])
        gather_out = Gather(links, here, R.out_weight.at[0], V, RO, pl.ds(0, D), local.at[1])
        core0, core1 = s == 0, s == 1
        gather_rows.start(core0)

        code_sends = []
        code_locals = []
        for at, key in enumerate(((R.step_codes, R.step), (R.decay_codes, R.decay))):
            ref, held = key
            item = links.transfer(
                lambda ref=ref: ref.at[0, 1 - s, 0], lambda held=held: held.at[s], here.other
            )
            item.start()
            code_sends.append(item)
            copy = pltpu.make_async_copy(ref.at[0, s, 0], held.at[s], local.at[2 + at])
            copy.start()
            code_locals.append(copy)
        hid_copy = pltpu.make_async_copy(R.inputs.at[s, 0], R.hid.at[0], local.at[4])
        hid_copy.start()
        cot_copy = pltpu.make_async_copy(R.out_grad.at[s, 0], R.cot.at[LAYERS], local.at[5])
        cot_copy.start()

        small = R.small_mine
        small[0] = jnp.zeros((8, DC), F32)
        wn, wc, wk, wg = D // OWNERS, DC // OWNERS, HEADS // OWNERS, DI // OWNERS
        small[0, 0:1, 0:wn] = R.norm_gain[...].astype(F32)
        small[0, 1:5, 0:wc] = R.conv_weight[0].astype(F32)
        small[0, 5:6, 0:wc] = R.conv_bias[...].astype(F32)
        skip = R.skip_gain[...].astype(F32)
        for head in range(wk):
            small[0, 6:7, head * HD : (head + 1) * HD] = jnp.broadcast_to(
                skip[:, head : head + 1], (1, HD)
            )
        small[0, 7:8, 0:wg] = R.gate_gain[...].astype(F32)
        raw = small[0]
        row = lax.broadcasted_iota(jnp.int32, (8, DC), 0)

        def turned(value, width, back):
            return pltpu.roll(value, lax.rem((DC - f * width if back else f * width), DC), 1)

        def by_row(value, back):
            out = turned(value, wc, back)
            out = jnp.where(row == 0, turned(value, wn, back), out)
            return jnp.where(row >= 6, turned(value, wg, back), out)

        small[0] = by_row(raw, False)
        small_steps = []
        for k, bit in enumerate(here.bits):
            item = links.transfer(
                lambda k=k: small.at[k], lambda k=k: R.small_in.at[k], here.to_owner(bit)
            )
            small_steps.append(item)
        small_core = links.transfer(
            lambda: R.params.at[s], lambda: R.params.at[s], here.other
        )
        small_steps[0].start()

        for copy in code_locals:
            copy.wait()
        for item in code_sends:
            item.arrived()
        lane = lax.broadcasted_iota(jnp.int32, (T, T), 1)
        sub = lax.broadcasted_iota(jnp.int32, (T, T), 0)
        causal = sub >= lane
        tri = jnp.where(causal, 1.0, 0.0).astype(F32)
        eye = jnp.where(sub == lane, 1.0, 0.0).astype(F32)
        spread = jnp.where(
            lax.broadcasted_iota(jnp.int32, (HEADS, DI), 1) // HD
            == lax.broadcasted_iota(jnp.int32, (HEADS, DI), 0),
            1.0,
            0.0,
        ).astype(F32)

        def prepare(layer):
            step_t = R.step[layer].astype(F32) / STEP_SCALE
            fall = R.decay[layer].astype(F32)
            cum = dot(tri, fall, NT, HIGHEST) / -DECAY_SCALE
            cum_t = dot(fall, tri, NT, HIGHEST) / -DECAY_SCALE
            steps = dot(eye, step_t, NT, HIGHEST)
            last = cum[T - 1 : T, :]
            R.ecum[layer] = dot(jnp.exp(cum), spread, precision=HIGHEST)
            R.toend[layer] = dot(jnp.exp(last - cum) * steps, spread, precision=HIGHEST)
            for head in range(HEADS):
                gap = cum[:, head : head + 1] - cum_t[head : head + 1, :]
                decays = jnp.where(causal, jnp.exp(jnp.where(causal, gap, 0.0)), 0.0)
                side = (head % 2) * T
                R.Dm[layer, head // 2, :, side : side + T] = decays * step_t[head : head + 1, :]

        prepare(0)
        gather_rows.advance(0, core0)
        gather_gates.start(core0)
        prepare(1)

        for k, item in enumerate(small_steps):
            item.arrived()
            total = small[k] + R.small_in[k]
            if k + 1 < len(small_steps):
                small[k + 1] = total
                small_steps[k + 1].start()
            else:
                R.params[s] = total
        small_core.start()
        small_core.arrived()
        hid_copy.wait()

        gather_rows.rest(core0)
        gather_rows.from_other(core1)

        low_lane = lane < HD

        def block_diag(pair):
            zero = jnp.zeros_like(pair)
            return jnp.concatenate(
                [jnp.where(low_lane, pair, zero), jnp.where(low_lane, zero, pair)], axis=0
            )

        def param(layer, name, cols, at=0):
            first = name + at
            return R.params[layer, first : first + 1, cols]

        def conv_argument(layer, cols):
            total = param(layer, BIAS, cols)
            for k in range(4):
                total = total + param(layer, TAPS, cols, k) * R.ext[
                    layer, HALO - 3 + k : HALO - 3 + k + T, cols
                ]
            return total

        def queries(layer):
            return R.act[layer, :, DI + N : DI + 2 * N]

        def input_keys(layer):
            return R.act[layer, :, DI : DI + N]

        share = [None] * LAYERS
        states = [None] * LAYERS

        def own_or_other(layer, src, out):
            item = links.transfer(lambda: src, lambda: out.at[0, s, 0], here.other)
            copy = lambda: pltpu.make_async_copy(src, out.at[0, s, 0], local.at[6])
            owner, guest = s == layer, s != layer
            when(owner, lambda: copy().start())
            item.start(guest)

            def end():
                when(owner, lambda: copy().wait())
                item.arrived(owner)

            return end

        def forward(layer, pump):
            pump(0)
            hid = R.hid
            u = hid[layer]
            inverse = lax.rsqrt(jnp.mean(u * u, axis=1, keepdims=True) + EPSILON)
            R.nrm[layer, mine_rows, :] = (
                u * inverse * param(layer, NORM, slice(0, D))
            ).astype(BF16)
            swap_nrm = links.transfer(
                lambda: R.nrm.at[layer, mine_rows, :],
                lambda: R.nrm.at[layer, mine_rows, :],
                here.other,
            )
            swap_nrm.start()

            def project(i):
                normed = R.nrm[layer, mine_rows, :]
                R.ext[layer, HALO : HALO + T, tile(i, 256)] = dot(
                    normed, W[layer, :, pl.ds(pl.multiple_of(DI + i * 256, 256), 256)]
                )

            loop(DC // 256, project)
            halo = links.transfer(
                lambda: R.ext.at[layer, T : T + HALO, :],
                lambda: R.ext.at[layer, 0:HALO, :],
                here.after,
            )
            halo.start(here.not_last)

            def clear():
                R.ext[layer, 0:HALO, :] = jnp.zeros((HALO, DC), F32)
                R.st[layer] = jnp.zeros((N, DI), BF16)

            when(here.first, clear)

            halo.arrived(here.not_first)

            def convolve(i):
                v = conv_argument(layer, tile(i, LANES))
                R.act[layer, :, tile(i, LANES)] = v * sigmoid(v)

            loop(DC // LANES, convolve)
            C, B = queries(layer), input_keys(layer)
            scores = dot(C, B, NT, HIGHEST)
            R.score[layer] = scores

            hand = []
            for g in range(GROUPS):
                cols = slice(g * GW, (g + 1) * GW)
                weighted = (R.act[layer, :, cols] * R.toend[layer, :, cols]).astype(BF16)
                R.part[:, cols] = dot2(B, weighted, TN)
                hand.append(
                    links.transfer(
                        lambda cols=cols: R.so.at[layer, :, cols],
                        lambda cols=cols: R.st.at[layer, :, cols],
                        here.after,
                    )
                )

            def first_sends():
                R.so[layer] = R.part[...].astype(BF16)
                for item in hand:
                    item.make().start()

            when(here.first, first_sends)
            pump(1)

            def gates(i):
                normed = R.nrm[layer, mine_rows, :]
                R.gate[layer, :, tile(i, 256)] = dot(normed, W[layer, :, tile(i, 256)])

            loop(DI // 256, gates)
            for g in range(GROUPS):
                for pair in range(g * PG, (g + 1) * PG):
                    cols = slice(pair * LANES, (pair + 1) * LANES)
                    dm = R.Dm[layer, pair]
                    both = jnp.concatenate([dm[:, :T] * scores, dm[:, T:] * scores], axis=1)
                    x = R.act[layer, :, cols]
                    R.mixed[layer, :, cols] = (
                        dot(both.astype(BF16), block_diag(x.astype(BF16)))
                        + param(layer, SKIP, cols) * x
                    )
                cols = slice(g * GW, (g + 1) * GW)

                def pass_on(g=g, cols=cols):
                    hand[g].make().wait_recv()
                    R.so[layer, :, cols] = (
                        R.part[:, cols]
                        + R.ecum[layer, T - 1 : T, cols] * R.st[layer, :, cols].astype(F32)
                    ).astype(BF16)

                when(here.not_first, pass_on)
                when(here.not_first & here.not_last, lambda g=g: hand[g].make().start())
                R.mixed[layer, :, cols] += R.ecum[layer, :, cols] * dot2(
                    C, R.st[layer, :, cols]
                )
                if g == GROUPS // 2:
                    pump(2)

            pump(3)

            def gating(i, squares):
                cols = tile(i, LANES)
                gate = R.gate[layer, :, cols]
                value = R.mixed[layer, :, cols] * (gate * sigmoid(gate))
                return squares + value * value

            squares = lax.fori_loop(0, DI // LANES, gating, jnp.zeros((T, LANES), F32))
            r2 = lax.rsqrt(jnp.sum(squares, axis=1, keepdims=True) / DI + EPSILON)
            R.r2[layer] = r2

            def scaled(i):
                cols = tile(i, LANES)
                gate = R.gate[layer, :, cols]
                value = R.mixed[layer, :, cols] * (gate * sigmoid(gate))
                R.no[layer, mine_rows, cols] = (
                    value * r2 * param(layer, GATE, cols)
                ).astype(BF16)

            loop(DI // LANES, scaled)
            swap_no = links.transfer(
                lambda: R.no.at[layer, mine_rows, :],
                lambda: R.no.at[layer, mine_rows, :],
                here.other,
            )
            swap_no.start()
            pump(4)

            def output(i):
                hid[layer + 1, :, tile(i, 256)] = hid[layer, :, tile(i, 256)] + dot(
                    R.no[layer, mine_rows, :], V[layer, :, tile(i, 256)]
                )

            loop(D // 256, output)
            share[layer] = types.SimpleNamespace(nrm=swap_nrm, no=swap_no)
            states[layer] = hand
            return own_or_other(layer, hid.at[layer + 1], R.o_res)

        def during_0(point):
            if point == 0:
                gather_gates.advance(0, core0)
                gather_out.start(core0)
            elif point == 1:
                gather_gates.rest(core0)
                gather_gates.from_other(core1)
                gather_rows.start(core1)
            elif point == 2:
                gather_out.advance(0, core0)
            elif point == 3:
                gather_gates.start(core1)
            else:
                gather_out.rest(core0)
                gather_out.from_other(core1)

        def during_1(point):
            if point == 0:
                gather_gates.advance(0, core1)
                gather_out.start(core1)
            elif point == 1:
                gather_gates.rest(core1)
                gather_gates.from_other(core0)
            elif point == 2:
                gather_out.advance(0, core1)
            elif point == 4:
                gather_out.rest(core1)
                gather_out.from_other(core0)

        ends = [forward(0, during_0)]
        gather_rows.advance(0, core1)
        gather_rows.rest(core1)
        gather_rows.from_other(core0)
        ends.append(forward(1, during_1))
        for end in ends:
            end()
        cot_copy.wait()

        def add_row(layer, name, cols, value, at=0):
            first = 8 * layer + name + at
            R.sums[first : first + 1, cols] = jnp.sum(value, axis=0, keepdims=True)

        def half_swap(layer, src, dst, width):
            item = links.transfer(
                lambda: src.at[:, pl.ds(pl.multiple_of((1 - s) * width, LANES), width)],
                lambda: dst.at[layer, mine_rows, :],
                here.other,
            )
            item.start()
            dst[layer, mine_rows, :] = src[:, pl.ds(pl.multiple_of(s * width, LANES), width)]
            return item

        R.sums[...] = jnp.zeros((2 * 8, DC), F32)

        def backward(layer, plan):
            plan = iter(plan)

            def pump():
                for action in next(plan):
                    action()

            hid, cot = R.hid, R.cot
            R.cbf[layer] = cot[layer + 1].astype(BF16)
            share[layer].cb = half_swap(layer, R.cbf.at[layer], R.cb2, OW)
            r2 = R.r2[layer]

            def first_pass(i, total):
                cols = tile(i, 256)
                d = dot(R.cbf[layer], V[layer, cols, :], NT)
                R.dno[:, cols] = d
                gate = R.gate[layer, :, cols]
                gated = R.mixed[layer, :, cols] * (gate * sigmoid(gate))
                add_row(layer, GATE, cols, d * gated * r2)
                return total + jnp.sum(
                    d * param(layer, GATE, cols) * gated, axis=1, keepdims=True
                )

            total = lax.fori_loop(0, DI // 256, first_pass, jnp.zeros((T, 1), F32))
            factor = r2 * r2 * r2 * total / DI
            pump()
            dproj = R.dproj.at[layer]

            def second_pass(i):
                cols = tile(i, LANES)
                gate = R.gate[layer, :, cols]
                sg = sigmoid(gate)
                dg = (
                    R.dno[:, cols] * param(layer, GATE, cols) * r2
                    - R.mixed[layer, :, cols] * (gate * sg) * factor
                )
                dm = dg * (gate * sg)
                R.dno[:, cols] = dm
                dproj[:, cols] = (
                    dg * R.mixed[layer, :, cols] * (sg * (1.0 + gate * (1.0 - sg)))
                ).astype(BF16)
                R.ed[:, cols] = dm * R.ecum[layer, :, cols]
                add_row(layer, SKIP, cols, dm * R.act[layer, :, cols])

            loop(DI // LANES, second_pass)
            share[layer].e = half_swap(layer, dproj, R.dE, EW)
            pump()
            C, B = queries(layer), input_keys(layer)
            for item in states[layer]:
                when(here.not_last, lambda item=item: item.make().wait_send())
            hand = []
            for g in range(GROUPS):
                cols = slice(g * GW, (g + 1) * GW)
                R.part[:, cols] = dot2(C, R.ed[:, cols].astype(BF16), TN)
                hand.append(
                    links.transfer(
                        lambda cols=cols: R.so.at[layer, :, cols],
                        lambda cols=cols: R.lv.at[layer, :, cols],
                        here.before,
                    )
                )

            def first_sends():
                R.lv[layer] = jnp.zeros((N, DI), BF16)
                R.dpx_in[layer] = jnp.zeros((HALO, DC), F32)
                R.so[layer] = R.part[...].astype(BF16)
                for item in hand:
                    item.make().start()

            when(here.last, first_sends)
            scores = R.score[layer]
            R.dsc[...] = jnp.zeros((T, T), F32)
            R.dB[...] = jnp.zeros((T, N), F32)
            R.dCq[...] = jnp.zeros((T, N), F32)
            for g in range(GROUPS):
                for pair in range(g * PG, (g + 1) * PG):
                    cols = slice(pair * LANES, (pair + 1) * LANES)
                    dm = R.dno[:, cols]
                    dmb = dm.astype(BF16)
                    decays = R.Dm[layer, pair]
                    x = R.act[layer, :, cols]
                    high = x.astype(BF16)
                    low = (x - high.astype(F32)).astype(BF16)
                    dc = dot2(dm, block_diag(high), NT) + dot(dmb, block_diag(low), NT)
                    R.dsc[...] += decays[:, :T] * dc[:, :T] + decays[:, T:] * dc[:, T:]
                    both = jnp.concatenate([decays[:, :T] * scores, decays[:, T:] * scores], axis=1)
                    back = dot(both.astype(BF16), dmb, TN)
                    R.dact[:, cols] = param(layer, SKIP, cols) * dm + jnp.where(
                        low_lane, back[:T], back[T:]
                    )
                cols = slice(g * GW, (g + 1) * GW)

                def pass_on(g=g, cols=cols):
                    hand[g].make().wait_recv()
                    R.so[layer, :, cols] = (
                        R.part[:, cols]
                        + R.ecum[layer, T - 1 : T, cols] * R.lv[layer, :, cols].astype(F32)
                    ).astype(BF16)

                when(here.not_last, pass_on)
                when(here.not_first & here.not_last, lambda g=g: hand[g].make().start())
                links.open.append((here.not_first, hand[g]))
                leaving = R.lv[layer, :, cols]
                toend = R.toend[layer, :, cols]
                R.dact[:, cols] += toend * dot2(B, leaving)
                R.dB[...] += dot2(R.act[layer, :, cols] * toend, leaving, NT)
                R.dCq[...] += dot2(R.ed[:, cols], R.st[layer, :, cols], NT)
                pump()
            dsc = R.dsc[...]
            R.dact[:, DI : DI + N] = R.dB[...] + dot(dsc, C, TN, HIGHEST)
            R.dact[:, DI + N :] = R.dCq[...] + dot(dsc, B, precision=HIGHEST)

            def conv_back(i):
                cols = tile(i, LANES)
                v = conv_argument(layer, cols)
                sg = sigmoid(v)
                d = R.dact[:, cols] * (sg * (1.0 + v * (1.0 - sg)))
                R.dpx[0:T, cols] = d
                R.dpx_out[layer, :, cols] = d[:HALO]
                add_row(layer, BIAS, cols, d)
                for k in range(4):
                    add_row(
                        layer,
                        TAPS,
                        cols,
                        d * R.ext[layer, HALO - 3 + k : HALO - 3 + k + T, cols],
                        k,
                    )

            loop(DC // LANES, conv_back)
            halo = links.transfer(
                lambda: R.dpx_out.at[layer],
                lambda: R.dpx_in.at[layer],
                here.before,
            )
            halo.start(here.not_first)
            pump()
            halo.arrived(here.not_last)
            R.dpx[T : T + HALO, :] = R.dpx_in[layer]

            def rows_back(i):
                cols = tile(i, LANES)
                total = param(layer, TAPS, cols, 3) * R.dpx[0:T, cols]
                for k in range(3):
                    total = total + param(layer, TAPS, cols, k) * R.dpx[
                        3 - k : 3 - k + T, cols
                    ]
                dproj[:, pl.ds(pl.multiple_of(DI + i * LANES, LANES), LANES)] = total.astype(BF16)

            loop(DC // LANES, rows_back)
            share[layer].l = half_swap(layer, R.dproj.at[layer, :, pl.ds(DI, DC)], R.dL, LW)
            pump()

            def normed_back(i):
                R.dnr[:, tile(i, 256)] = dot(dproj[...], W[layer, tile(i, 256), :], NT)

            loop(D // 256, normed_back)
            pump()
            u = hid[layer]
            inverse = lax.rsqrt(jnp.mean(u * u, axis=1, keepdims=True) + EPSILON)
            dn = R.dnr[...]
            add_row(layer, NORM, slice(0, D), dn * u * inverse)
            da = dn * param(layer, NORM, slice(0, D))
            pull = jnp.sum(da * u, axis=1, keepdims=True)
            cot[layer] = (
                cot[layer + 1] + da * inverse - u * (inverse * inverse * inverse * pull / D)
            )
            return own_or_other(layer, cot.at[layer], R.o_grad)

        def out_grads(layer):
            share[layer].no.arrived()
            share[layer].cb.arrived()

            def part(i):
                value = dot(R.no[layer, :, tile(i, 256)], R.cb2[layer], TN).astype(BF16)
                R.g[OUT_A][layer, tile(i, 256), :] = value[:, :OA]
                R.g[OUT_B][layer, tile(i, 256), :] = value[:, OA:]

            loop(DI // 256, part)

        def in_grads(layer, came, right, a, b):
            came.arrived()

            def part(i):
                value = dot(R.nrm[layer, :, tile(i, 256)], right[layer], TN).astype(BF16)
                split = R.g[a].shape[-1]
                R.g[a][layer, tile(i, 256), :] = value[:, :split]
                R.g[b][layer, tile(i, 256), :] = value[:, split:]

            loop(D // 256, part)

        def gate_grads(layer):
            share[layer].nrm.arrived()
            in_grads(layer, share[layer].e, R.dE, E_A, E_B)

        def row_grads(layer):
            in_grads(layer, share[layer].l, R.dL, L_A, L_B)

        class Reduce:
            def __init__(self, layer, key, order, cols, out):
                self.layer, self.order = layer, order
                rows, width = SIZES[key]
                self.rows = rows
                self.g = R.g[key].at[layer]
                rx = R.rx[key].at[layer]
                self.phases = []
                slot = 0
                for k, bit in enumerate(order):
                    masks = [0]
                    for rest in order[k + 1 :]:
                        masks = masks + [m ^ rest for m in masks]
                    phase = []
                    for mask in masks:
                        item = links.transfer(
                            lambda bit=bit, mask=mask: self.g.at[self.block(bit ^ mask), :],
                            lambda slot=slot: rx.at[slot],
                            here.to_owner(bit),
                        )
                        phase.append((item, mask, rx.at[slot]))
                        slot += 1
                    self.phases.append(phase)
                self.fold = Fold(
                    links, here, None, self.g.at[self.block(0), :], R.up[key].at[layer],
                    R.tin[key].at[layer], rx.at[slot - 1],
                )
                total = rx.at[slot - 1]
                place = lambda: out.at[
                    :, pl.ds(pl.multiple_of(cols[0] + s * cols[1], LANES), width)
                ]
                self.owner, self.guest = s == layer, s != layer
                self.out = links.transfer(lambda: total, place, here.other)
                sem = local.at[8 + 6 * layer + key]
                self.local = lambda: pltpu.make_async_copy(total, place(), sem)
                self.chunk = 32 if rows % 32 == 0 else 16

            def block(self, mask):
                return pl.ds(pl.multiple_of(here.owner(mask) * self.rows, self.rows), self.rows)

            def piece(self, i, start=0):
                return pl.ds(pl.multiple_of(start + i * self.chunk, self.chunk), self.chunk)

            def start(self):
                for item, _, _ in self.phases[0]:
                    item.start()

            def advance(self, k):
                for item, mask, got in self.phases[k]:
                    item.arrived()

                    def add(i, mask=mask, got=got):
                        at = self.piece(i, here.owner(mask) * self.rows)
                        self.g[at, :] = (
                            self.g[at, :].astype(F32) + got[self.piece(i), :].astype(F32)
                        ).astype(BF16)

                    loop(self.rows // self.chunk, add)
                for item, _, _ in self.phases[k + 1]:
                    item.start()

            def put(self, extra):
                (item, _, got), = self.phases[-1]
                item.arrived()

                def add(i):
                    at = self.piece(i, f * self.rows)
                    value = self.g[at, :].astype(F32) + got[self.piece(i), :].astype(F32)
                    if extra is not None:
                        value = value + extra[self.piece(i), :].astype(F32)
                    self.g[at, :] = value.astype(BF16)

                loop(self.rows // self.chunk, add)

            def both(self, dst, a, b):
                def add(i):
                    dst[self.piece(i), :] = (
                        self.g[self.piece(i, f * self.rows), :].astype(F32)
                        + b[self.piece(i), :].astype(F32)
                    ).astype(BF16)

                loop(self.rows // self.chunk, add)

            def copy(self, dst, a):
                def move(i):
                    dst[self.piece(i), :] = a[self.piece(i), :]

                loop(self.rows // self.chunk, move)

            def deliver(self, condition):
                when(self.owner & condition, lambda: self.local().start())
                self.out.start(self.guest & condition)

            def begin(self):
                self.fold.begin(self.put)

            def collect(self):
                self.fold.collect(self.put)

            def turn(self):
                self.fold.turn(self.both)
                self.deliver(self.fold.middle)

            def settle(self):
                self.fold.settle(self.copy)
                self.deliver(self.fold.outer)

            def end(self):
                when(self.owner, lambda: self.local().wait())
                self.out.arrived(self.owner)

        class Both:
            def __init__(self, *items):
                self.items = items

            def start(self):
                for item in self.items:
                    item.start()

            def advance(self):
                for k in range(len(here.bits) - 1):
                    for item in self.items:
                        item.advance(k)

            def begin(self):
                for item in self.items:
                    item.begin()

            def collect(self):
                for item in self.items:
                    item.collect()

            def turn(self):
                for item in self.items:
                    item.turn()

            def settle(self):
                for item in self.items:
                    item.settle()

            def end(self):
                for item in self.items:
                    item.end()

        straight, backwards = here.bits, here.bits[::-1]
        out, gates_in, rows_in = [], [], []
        for layer in range(LAYERS):
            out.append(
                Both(
                    Reduce(layer, OUT_A, straight, (0, OW), R.o_out),
                    Reduce(layer, OUT_B, backwards, (OA, OW), R.o_out),
                )
            )
            gates_in.append(
                Both(
                    Reduce(layer, E_A, backwards, (0, EW), R.o_in),
                    Reduce(layer, E_B, straight, (EA, EW), R.o_in),
                )
            )
            rows_in.append(
                Both(
                    Reduce(layer, L_A, straight, (DI, LW), R.o_in),
                    Reduce(layer, L_B, backwards, (DI + LA, LW), R.o_in),
                )
            )

        plan1 = (
            [lambda: out_grads(1), out[1].start],
            [],
            [lambda: gate_grads(1), gates_in[1].start],
            [],
            [],
            [out[1].advance],
            [],
            [],
            [gates_in[1].advance],
            [lambda: row_grads(1), rows_in[1].start, out[1].begin],
            [],
        )
        plan0 = (
            [lambda: out_grads(0), out[0].start, gates_in[1].begin],
            [out[1].collect],
            [lambda: gate_grads(0), gates_in[0].start],
            [rows_in[1].advance],
            [out[1].turn, gates_in[1].collect],
            [],
            [out[0].advance],
            [rows_in[1].begin, gates_in[1].turn],
            [gates_in[0].advance],
            [lambda: row_grads(0), rows_in[0].start, out[1].settle],
            [out[0].begin, rows_in[1].collect, gates_in[1].settle],
        )
        ends = [backward(1, plan1), backward(0, plan0)]

        theirs = pl.ds(pl.multiple_of((1 - s) * 8, 8), 8)
        sums_core = links.transfer(lambda: R.sums.at[theirs, :], lambda: R.sums_core, here.other)
        sums_core.start()
        steps = [
            links.transfer(
                lambda k=k: R.sums_mine.at[k], lambda k=k: R.sums_in.at[k], here.to_owner(bit)
            )
            for k, bit in enumerate(here.bits)
        ]
        small_fold = Fold(
            links, here, None, R.sums_mine.at[len(here.bits)], R.sums_up, R.sums_tin, R.sums_total
        )

        def small_put(extra):
            k = len(here.bits) - 1
            steps[k].arrived()
            value = R.sums_mine[k] + R.sums_in[k]
            R.sums_mine[k + 1] = value if extra is None else value + extra[...]

        def small_both(dst, a, b):
            dst[...] = a[...] + b[...]

        def small_copy(dst, a):
            dst[...] = a[...]

        sums_core.arrived()
        R.sums_mine[0] = R.sums[pl.ds(pl.multiple_of(s * 8, 8), 8), :] + R.sums_core[...]
        steps[0].start()
        gates_in[0].begin()
        rows_in[0].advance()
        for k in range(len(here.bits) - 1):
            steps[k].arrived()
            R.sums_mine[k + 1] = R.sums_mine[k] + R.sums_in[k]
            steps[k + 1].start()
        out[0].collect()
        rows_in[1].turn()
        small_fold.begin(small_put)
        rows_in[0].begin()
        gates_in[0].collect()
        small_fold.collect(small_put)
        out[0].turn()
        rows_in[1].settle()
        rows_in[0].collect()
        gates_in[0].turn()
        small_fold.turn(small_both)
        out[0].settle()
        rows_in[0].turn()
        gates_in[0].settle()
        small_fold.settle(small_copy)
        rows_in[0].settle()
        total = R.sums_total[...]
        R.o_small[...] = by_row(total, True)[:, : R.o_small.shape[1]]
        for item in out + gates_in + rows_in:
            item.end()
        for end in ends:
            end()
        links.close()

    return kernel, list(scratch.values()) + sum(sums, [])


def body(
    inputs,
    out_grad,
    norm_gain,
    input_weight,
    conv_weight,
    conv_bias,
    skip_gain,
    gate_gain,
    out_weight,
    step_codes,
    decay_codes,
):
    given = types.SimpleNamespace(**locals())
    names = tuple(vars(given))
    owners, seq = lax.axis_size("fsdp"), lax.axis_size("seq")
    assert lax.axis_size("section") == 2 and owners & (owners - 1) == 0 and owners > 1
    T, D = given.inputs.shape[2:]
    rows_in, PROJ = given.input_weight.shape[1:]
    rows_out = given.out_weight.shape[1]
    DI = rows_out * owners
    HEADS = given.step_codes.shape[-1]
    given.step_codes = jnp.swapaxes(step_codes, -1, -2)
    given.decay_codes = jnp.swapaxes(decay_codes, -1, -2)
    arrays = tuple(vars(given).values())
    dims = types.SimpleNamespace(
        T=T, D=D, PROJ=PROJ, DI=DI, HEADS=HEADS, OWNERS=owners, seq=seq,
        NBITS=owners.bit_length() - 1,
    )
    kernel, scratch = make_body(dims, names)
    vmem = pl.BlockSpec(memory_space=pltpu.VMEM)
    hbm = pl.BlockSpec(memory_space=pl.ANY)
    small_width = -(-(PROJ - DI) // owners // LANES) * LANES
    part = (1, given.inputs.shape[0], 1, T, D)
    out_shape = (
        jax.ShapeDtypeStruct(part, F32),
        jax.ShapeDtypeStruct(part, F32),
        jax.ShapeDtypeStruct((rows_in, PROJ), BF16),
        jax.ShapeDtypeStruct((rows_out, D), BF16),
        jax.ShapeDtypeStruct((8, small_width), F32),
    )
    results, gradients, grad_in, grad_out, small = pl.pallas_call(
        kernel,
        out_shape=out_shape,
        in_specs=[hbm if array.ndim > 3 and array.dtype == F32 or array.size > 2**17 else vmem for array in arrays],
        out_specs=(hbm, hbm, hbm, hbm, vmem),
        scratch_shapes=[pltpu.VMEM(shape, dtype) for shape, dtype in scratch]
        + [
            pltpu.SemaphoreType.DMA((TRANSFERS,)),
            pltpu.SemaphoreType.DMA((TRANSFERS,)),
            pltpu.SemaphoreType.DMA((24,)),
        ],
        compiler_params=pltpu.CompilerParams(
            collective_id=0, has_side_effects=True, vmem_limit_bytes=63 * 2**20
        ),
    )(*arrays)
    wn, wc, wg = given.norm_gain.shape[1], given.conv_bias.shape[1], rows_out
    heads = given.skip_gain.shape[1]
    return (
        results,
        gradients,
        small[0:1, :wn],
        grad_in.astype(F32)[None],
        small[1:5, :wc][None],
        small[5:6, :wc],
        small[6, :wg].reshape(1, heads, -1).sum(axis=-1),
        small[7:8, :wg],
        grad_out.astype(F32)[None],
    )


def solution(mesh):
    return jax.shard_map(
        body,
        mesh=mesh,
        in_specs=(
            P(None, "fsdp", "seq", None),
            P(None, "fsdp", "seq", None),
            P("section", "fsdp"),
            P("section", "fsdp", None),
            P("section", None, "fsdp"),
            P("section", "fsdp"),
            P("section", "fsdp"),
            P("section", "fsdp"),
            P("section", "fsdp", None),
            P("section", None, "fsdp", "seq", None),
            P("section", None, "fsdp", "seq", None),
        ),
        out_specs=(
            P("section", None, "fsdp", "seq", None),
            P("section", None, "fsdp", "seq", None),
            P("section", "fsdp"),
            P("section", "fsdp", None),
            P("section", None, "fsdp"),
            P("section", "fsdp"),
            P("section", "fsdp"),
            P("section", "fsdp"),
            P("section", "fsdp", None),
        ),
        check_vma=False,
    )
```
